128 devices in a mesh: gauss: 32 (over z, x, core), pix: 4 (over y).
Axes of the slice: x: 4, y: 4, z: 4, core: 2. Of those that a mesh axis runs over, the one named last changes fastest.
Arguments:
- gauss_fields: float32 [9, 1048576], P(None, ('gauss', 'pix')), may hold values from -4 to 532, as said below
- send_rows: int32 [128, 128, 64], P(('gauss', 'pix')), may hold values from 0 to 8191, as said below
- tile_list: int32 [1024, 256], P(('gauss', 'pix')), may hold values from 0 to 8191, as said below
- tile_count: int32 [1024], P(('gauss', 'pix')), may hold values from 1 to 256, as said below
- pixel_grad: float32 [1024, 3, 256], P(('gauss', 'pix')), may hold values from -6 to 6
Outputs:
- field_grads: float32 [9, 1048576], P(None, ('gauss', 'pix'))
The draws below stay inside these ranges and needn't reach their ends.
Inputs may be any that keep to these rules, and one draw needn't show every extreme that they name: For each s and d the entries send_rows[s, d, :] are distinct, every one of them equals d modulo 128, and no row of s is sent to two devices. `tile_list`: entries of one tile's list are distinct. `tile_count`: A tile's entries beyond its count are padding. Every tile of one device has exactly 256 live entries. `gauss_fields`: conic a and c are positive and b * b < a * c. Opacities lie in 0.004 to 0.035, colors in 0 to 1.
All inputs are finite; a program needn't handle non-finite values.
Results may differ from the reference program's by a relative error of at most 0.0003.
Values sent between devices are 32-bit elements; how exact they have to be, the bound alone decides.
No kernel may reach another device: no remote copies, remote signals or barrier semaphores. Data moves between devices by JAX's collectives and lax.ppermute only.
A program may use at most 64 MiB of HBM per device.

```python
import math
import jax
import jax.numpy as jnp
from jax import lax

FIELDS = 9
TILE_PIX = 256
TILES_X = 32
TILES_Y = 8
LIST = 256
G_DEV = 8192
TILES_DEV = 8
CAP = 64
GAUSS = 1048576
TILES = 1024
DEVICES = 128


def shared_rows(key):
    inner_key = jax.random.fold_in(key, 101)
    per_pair = G_DEV // DEVICES
    scores = jax.random.randint(inner_key, (DEVICES, DEVICES, per_pair), 0, 65536) * per_pair
    scores = scores + jnp.arange(per_pair, dtype=jnp.int32)[None, None, :]
    _, picked = lax.top_k(scores, CAP)
    receivers = jnp.arange(DEVICES, dtype=jnp.int32)[None, :, None]
    return (receivers + DEVICES * picked.astype(jnp.int32)).astype(jnp.int32)


def shared_home(key):
    inner_key = jax.random.fold_in(key, 202)
    offsets = jax.random.randint(inner_key, (DEVICES, G_DEV), 0, TILES_DEV)
    receivers = jnp.arange(G_DEV, dtype=jnp.int32) % DEVICES
    return (receivers[None, :] * TILES_DEV + offsets).astype(jnp.int32)


def draw_send_rows(key, part):
    return shared_rows(key)


def draw_tile_list(key, part):
    rows = shared_rows(key)
    home = shared_home(key)
    buffer_size = DEVICES * CAP
    list_key = jax.random.fold_in(key, 303)

    def per_device(device):
        rows_here = rows[:, device, :]
        slot_home = jnp.take_along_axis(home, rows_here, axis=1).reshape(-1)
        tiles_here = device * TILES_DEV + jnp.arange(TILES_DEV, dtype=jnp.int32)
        tile_col = tiles_here % TILES_X
        tile_row = tiles_here // TILES_X % TILES_Y
        tile_view = tiles_here // (TILES_X * TILES_Y)
        slot_col = slot_home % TILES_X
        slot_row = slot_home // TILES_X % TILES_Y
        slot_view = slot_home // (TILES_X * TILES_Y)
        near = (jnp.abs(tile_col[:, None] - slot_col[None, :]) <= 1) & (jnp.abs(tile_row[:, None] - slot_row[None, :]) <= 1) & (tile_view[:, None] == slot_view[None, :])
        base = jax.random.randint(jax.random.fold_in(list_key, device), (TILES_DEV, buffer_size), 0, 1024)
        scores = (base + 1024 * near.astype(jnp.int32)) * buffer_size + jnp.arange(buffer_size, dtype=jnp.int32)[None, :]
        _, picked = lax.top_k(scores, LIST)
        return picked.astype(jnp.int32)
    lists = lax.map(per_device, jnp.arange(DEVICES, dtype=jnp.int32))
    return lists.reshape(TILES, LIST).astype(jnp.int32)


def draw_gauss_fields(key, part):
    subkeys = jax.random.split(key, 7)
    home = shared_home(key).reshape(-1)
    gauss_total = G_DEV * DEVICES
    home_col = (home % TILES_X).astype(jnp.float32)
    home_row = (home // TILES_X % TILES_Y).astype(jnp.float32)
    centre_x = 16.0 * home_col + jax.random.uniform(subkeys[0], (gauss_total,), jnp.float32, -4.0, 20.0)
    centre_y = 16.0 * home_row + jax.random.uniform(subkeys[1], (gauss_total,), jnp.float32, -4.0, 20.0)
    sigma_a = jnp.exp(jax.random.uniform(subkeys[2], (gauss_total,), jnp.float32, math.log(4.0), math.log(24.0)))
    sigma_c = jnp.exp(jax.random.uniform(subkeys[3], (gauss_total,), jnp.float32, math.log(4.0), math.log(24.0)))
    conic_a = 1.0 / (sigma_a * sigma_a)
    conic_c = 1.0 / (sigma_c * sigma_c)
    correlation = jax.random.uniform(subkeys[4], (gauss_total,), jnp.float32, -0.7, 0.7)
    conic_b = correlation * jnp.sqrt(conic_a * conic_c)
    colors = jax.random.uniform(subkeys[5], (3, gauss_total), jnp.float32, 0.0, 1.0)
    opacity = jnp.exp(jax.random.uniform(subkeys[6], (gauss_total,), jnp.float32, math.log(0.004), math.log(0.035)))
    stacked = jnp.concatenate([centre_x[None], centre_y[None], conic_a[None], conic_b[None], conic_c[None], colors, opacity[None]], axis=0)
    return stacked.astype(jnp.float32)


def draw_tile_count(key, part):
    subkeys = jax.random.split(jax.random.fold_in(key, 404), 3)
    shifts = jax.random.randint(subkeys[0], (DEVICES,), 0, 3)
    heavy = jax.random.randint(subkeys[1], (), 0, DEVICES)
    ceiling = jnp.right_shift(jnp.full((DEVICES,), LIST, jnp.int32), shifts.astype(jnp.int32))
    ceiling_tiles = jnp.repeat(ceiling, TILES_DEV)
    counts = jax.random.randint(subkeys[2], (TILES,), 1, ceiling_tiles + 1)
    tile_owner = jnp.arange(TILES, dtype=jnp.int32) // TILES_DEV
    counts = jnp.where(tile_owner == heavy, LIST, counts)
    return counts.astype(jnp.int32)


def steps_of(own_key, extent, cuts, smallest, high):
    loudness = 1.0
    for dim, parts in cuts:
        draws = jax.random.uniform(jax.random.fold_in(jax.random.fold_in(own_key, 6), dim), (parts,), jnp.float32, smallest / len(cuts), high / len(cuts))
        loudness = loudness * jnp.repeat(jnp.exp(draws), extent[dim] // parts).reshape((-1,) + (1,) * (len(extent) - 1 - dim))
    return loudness


def noise(rng, dims, width, limit, pieces=(), kind=jnp.bfloat16):
    values = jax.random.normal(rng, dims, jnp.float32) * width
    if len(pieces) > 0:
        values = steps_of(rng, dims, pieces, -0.22, 0.18) * values
    return jnp.clip(values, min=-limit, max=limit).astype(kind)


def setup_inputs(seed: int = 0) -> dict:
    splits = jax.random.split(jax.random.key(seed), 6)
    return {
        "gauss_fields": draw_gauss_fields(jax.random.fold_in(splits[5], 71), 0),
        "send_rows": draw_send_rows(jax.random.fold_in(splits[5], 71), 0),
        "tile_list": draw_tile_list(jax.random.fold_in(splits[5], 71), 0),
        "tile_count": draw_tile_count(jax.random.fold_in(splits[5], 71), 0),
        "pixel_grad": noise(splits[4], (TILES, 3, TILE_PIX), 1.0, 6.0, ((0, 128),), jnp.float32),
    }


def tile_color(values, list_count, anchor_x, anchor_y):
    slots = values.shape[1]
    pixel_lane = jnp.arange(256)
    pixel_x = anchor_x + (pixel_lane % 16).astype(jnp.float32) + 0.5
    pixel_y = anchor_y + (pixel_lane // 16).astype(jnp.float32) + 0.5
    delta_x = pixel_x[None, :] - values[0][:, None]
    delta_y = pixel_y[None, :] - values[1][:, None]
    exponent = values[2][:, None] * delta_x * delta_x + 2.0 * values[3][:, None] * delta_x * delta_y + values[4][:, None] * delta_y * delta_y
    live_mask = (jnp.arange(slots) < list_count).astype(jnp.float32)
    opacity_term = (live_mask * values[8])[:, None] * jnp.exp(-0.5 * exponent)
    kept_light = jnp.cumprod(1.0 - opacity_term, axis=0)
    transmit = jnp.concatenate([jnp.ones((1, 256), jnp.float32), kept_light[:-1]], axis=0)
    weight = transmit * opacity_term
    return lax.optimization_barrier(jnp.sum(values[5:8][:, :, None] * weight[None, :, :], axis=1))

def tile_grad(values, list_count, tile_id, pixel_part):
    anchor_x = (tile_id % TILES_X * 16).astype(jnp.float32)
    anchor_y = (tile_id // TILES_X % TILES_Y * 16).astype(jnp.float32)
    _, pullback = jax.vjp(lambda inner: tile_color(inner, list_count, anchor_x, anchor_y), values)
    return pullback(pixel_part)[0]

def reference(gauss_fields, send_rows, tile_list, tile_count, pixel_grad):
    tile_ids = jnp.arange(TILES, dtype=jnp.int32)

    def per_tile(packed):
        tile_id, entries, list_count, pixel_part = packed
        receiver = tile_id // TILES_DEV
        source = entries // CAP
        slot_index = entries % CAP
        gauss_ids = (source * G_DEV + send_rows[source, receiver, slot_index]).astype(jnp.int32)
        gathered = jnp.take(gauss_fields, gauss_ids, axis=1)
        return (tile_grad(gathered, list_count, tile_id, pixel_part), gauss_ids)
    tile_grads, gauss_ids = lax.map(per_tile, (tile_ids, tile_list, tile_count, pixel_grad))
    flat_grads = jnp.moveaxis(tile_grads, 0, 1).reshape(FIELDS, -1)
    totals = jnp.zeros((FIELDS, GAUSS), jnp.float32)
    return totals.at[:, gauss_ids.reshape(-1)].add(flat_grads)
```

```python
import jax
import jax.numpy as jnp
from jax import lax
from jax.experimental import pallas as pl
from jax.experimental.pallas import tpu as pltpu
from jax.sharding import PartitionSpec as P

AXES = ("gauss", "pix")
TILES_X = 32
TILES_Y = 8
LOG2E = 1.4426950408889634
F32 = jnp.float32
BF16 = jnp.bfloat16


def split2(x):
    hi = x.astype(BF16)
    return hi, (x - hi.astype(F32)).astype(BF16)


def split3(x):
    hi = x.astype(BF16)
    rest = x - hi.astype(F32)
    mid = rest.astype(BF16)
    return hi, mid, (rest - mid.astype(F32)).astype(BF16)


def dot(a, b):
    return jnp.dot(a, b, preferred_element_type=F32)


def iota(shape, dim):
    return lax.broadcasted_iota(jnp.int32, shape, dim)


def tile_kernel(
    dev_ref, count_ref, recv_ref, list_ref, pg_ref, out_ref,
    rows_hm, rows_lo, tri_lt, tri_gt, basis, expo, logs, prod, gw, hh, acc,
):
    tiles = list_ref.shape[0]
    turned = recv_ref[...].T
    hi, mid, lo = split3(turned)
    rows_hm[:, 0:128] = hi
    rows_hm[:, 128:256] = mid
    rows_lo[...] = lo[0:576]
    before = (iota((256, 256), 0) < iota((256, 256), 1)).astype(F32).astype(BF16)
    after = (iota((256, 256), 0) > iota((256, 256), 1)).astype(F32).astype(BF16)
    tri_lt[0:256] = before
    tri_lt[256:512] = before
    tri_gt[0:256] = after
    tri_gt[256:512] = after
    pix = iota((16, 256), 1)
    u = (pix % 16).astype(F32) - 7.5
    v = (pix // 16).astype(F32) - 7.5
    which = iota((16, 256), 0)
    moments = jnp.where(which == 0, 1.0, 0.0)
    moments = jnp.where(which == 1, u, moments)
    moments = jnp.where(which == 2, v, moments)
    moments = jnp.where(which == 3, u * u, moments)
    moments = jnp.where(which == 4, u * v, moments)
    moments = jnp.where(which == 5, v * v, moments)
    moments = moments.astype(BF16)
    basis[:, 0:256] = moments
    basis[:, 256:512] = moments
    acc[...] = jnp.zeros_like(acc)
    first_tile = dev_ref[0] * tiles
    slot_row = iota((64, 256), 0)
    source_row = iota((128, 256), 0)

    def one_tile(t, carry):
        tile = first_tile + t
        anchor_x = (tile % TILES_X * 16).astype(F32)
        anchor_y = (tile // TILES_X % TILES_Y * 16).astype(F32)
        entry = list_ref[pl.ds(t, 1), :]
        one_source = (source_row == entry // 64).astype(F32).astype(BF16)
        two_source = jnp.concatenate([one_source, one_source], axis=0)

        def field(f, mask):
            found = dot(rows_hm[64 * f : 64 * f + 64, :], two_source)
            if f < 9:
                found = found + dot(rows_lo[64 * f : 64 * f + 64, :], one_source)
            return jnp.sum(jnp.where(mask, found, 0.0), axis=0, keepdims=True)

        row_of = field(9, slot_row == entry % 64)
        row_mask = slot_row == row_of.astype(jnp.int32)
        cx, cy, a, b, c, red, green, blue, opacity = [field(f, row_mask) for f in range(9)]

        side = iota((16, 256), 0).astype(F32) + 0.5
        dx = (anchor_x + side) - cx
        dy = (anchor_y + side) - cy
        live = iota((1, 256), 1) < count_ref[t]
        lead = jnp.where(live, jnp.log2(opacity), -100000.0)
        qa = (-0.5 * LOG2E) * a * dx * dx
        qb = -LOG2E * b * dx
        qc = (-0.5 * LOG2E) * c * dy * dy + lead
        for r in range(16):
            at = slice(16 * r, 16 * r + 16)
            e = qa + (qb * dy[r : r + 1, :] + qc[r : r + 1, :])
            alpha = jnp.exp2(e)
            expo[at, :] = e
            log_kept = jnp.log2(1.0 - alpha)
            prod[at, :] = log_kept
            lhi, llo = split2(log_kept)
            logs[at, 0:256] = lhi
            logs[at, 256:512] = llo

        rgb = jnp.concatenate([red, green, blue], axis=0)
        chi, cmid, clo = split3(rgb)
        phi, pmid, plo = split3(pg_ref[t])
        zero7 = jnp.zeros((14, 256), BF16)
        colors = jnp.concatenate([chi, cmid, clo, chi, cmid, chi, zero7], axis=0)
        lights = jnp.concatenate([phi, phi, phi, pmid, pmid, plo, zero7], axis=0)
        g = lax.dot_general(lights, colors, (((0,), (0,)), ((), ())), preferred_element_type=F32)

        transmit = jnp.exp2(dot(logs[...], tri_lt[...]))
        e = expo[...]
        w = transmit * jnp.exp2(e)
        whi, wlo = split2(w)
        gw_f = g * w
        ghi, glo = split2(gw_f)
        gw[:, 0:256] = ghi
        gw[:, 256:512] = glo
        behind = dot(gw[...], tri_gt[...])
        h = gw_f - behind * jnp.exp2(e - prod[...])
        hhi, hlo = split2(h)

        lit = jnp.concatenate([phi, pmid, plo, jnp.zeros((7, 256), BF16)], axis=0)
        rw = dot(lit, whi) + dot(lit, wlo)
        rh = dot(basis[:, 0:256], hhi) + dot(basis[:, 0:256], hlo)
        d_red = rw[0:1] + rw[3:4] + rw[6:7]
        d_green = rw[1:2] + rw[4:5] + rw[7:8]
        d_blue = rw[2:3] + rw[5:6] + rw[8:9]
        n00, n10, n01, n20, n11, n02 = [rh[m : m + 1] for m in range(6)]
        cu = cx - (anchor_x + 8.0)
        cv = cy - (anchor_y + 8.0)
        m10 = n10 - cu * n00
        m01 = n01 - cv * n00
        m20 = n20 - cu * (n10 + m10)
        m11 = n11 - cu * n01 - cv * m10
        m02 = n02 - cv * (n01 + m01)
        grads = [
            a * m10 + b * m01,
            b * m10 + c * m01,
            -0.5 * m20,
            -m11,
            -0.5 * m02,
            d_red,
            d_green,
            d_blue,
            n00 / opacity,
        ]
        row_one = row_mask.astype(F32)
        for f in range(9):
            yhi, ylo = split2(row_one * grads[f])
            acc[64 * f : 64 * f + 64, :] += lax.dot_general(
                jnp.concatenate([yhi, ylo], axis=1),
                jnp.concatenate([one_source, one_source], axis=1),
                (((1,), (1,)), ((), ())),
                preferred_element_type=F32,
            )
        return carry

    lax.fori_loop(0, tiles, one_tile, 0)
    out_ref[...] = acc[...].T


def tile_work(device, tile_count, received, tile_list, pixel_grad, interpret=False):
    smem = pl.BlockSpec(memory_space=pltpu.SMEM)
    vmem = pl.BlockSpec(memory_space=pltpu.VMEM)
    return pl.pallas_call(
        tile_kernel,
        out_shape=jax.ShapeDtypeStruct((128, 576), F32),
        in_specs=[smem, smem, vmem, vmem, vmem],
        out_specs=vmem,
        scratch_shapes=[
            pltpu.VMEM((640, 256), BF16),
            pltpu.VMEM((576, 128), BF16),
            pltpu.VMEM((512, 256), BF16),
            pltpu.VMEM((512, 256), BF16),
            pltpu.VMEM((16, 512), BF16),
            pltpu.VMEM((256, 256), F32),
            pltpu.VMEM((256, 512), BF16),
            pltpu.VMEM((256, 256), F32),
            pltpu.VMEM((256, 512), BF16),
            pltpu.VMEM((256, 512), BF16),
            pltpu.VMEM((576, 128), F32),
        ],
        name="splat_tiles",
        interpret=interpret,
    )(device, tile_count, received, tile_list, pixel_grad)


def on_device(gauss_fields, send_rows, tile_list, tile_count, pixel_grad):
    devices = lax.axis_size(AXES)
    rows = (send_rows[0] // devices).astype(F32)
    outgoing = jnp.concatenate([gauss_fields.reshape(576, devices).T, rows], axis=1)
    received = lax.all_to_all(outgoing, AXES, split_axis=0, concat_axis=0, tiled=True)
    device = lax.axis_index(AXES).reshape(1).astype(jnp.int32)
    grads = tile_work(device, tile_count, received, tile_list, pixel_grad)
    returned = lax.all_to_all(grads, AXES, split_axis=0, concat_axis=0, tiled=True)
    return returned.T.reshape(gauss_fields.shape)


def solution(mesh):
    placed = (
        P(None, AXES),
        P(AXES, None, None),
        P(AXES, None),
        P(AXES),
        P(AXES, None, None),
    )
    return jax.shard_map(
        on_device, mesh=mesh, in_specs=placed, out_specs=P(None, AXES), check_vma=False
    )
```

```python
import jax
import jax.numpy as jnp
from jax import lax
from jax.experimental import pallas as pl
from jax.experimental.pallas import tpu as pltpu
from jax.sharding import PartitionSpec as P

AXES = ("gauss", "pix")
TILES_X = 32
TILES_Y = 8
LOG2E = 1.4426950408889634
F32 = jnp.float32
BF16 = jnp.bfloat16
UNROLL = 2


def split2(x):
    hi = x.astype(BF16)
    return hi, (x - hi.astype(F32)).astype(BF16)


def split3(x):
    hi = x.astype(BF16)
    rest = x - hi.astype(F32)
    mid = rest.astype(BF16)
    return hi, mid, (rest - mid.astype(F32)).astype(BF16)


def dot(a, b):
    return jnp.dot(a, b, preferred_element_type=F32)


def iota(shape, dim):
    return lax.broadcasted_iota(jnp.int32, shape, dim)


def pack_kernel(fields_ref, rows_ref, out_ref, grid_ref):
    for p in range(64):
        grid_ref[pl.ds(p, 9, stride=64), :] = fields_ref[:, 128 * p : 128 * p + 128]
    grid_ref[576:640, :] = (rows_ref[...] // 128).astype(F32)
    for q in range(5):
        out_ref[pl.ds(q, 128, stride=5), :] = grid_ref[128 * q : 128 * q + 128, :].T


def unpack_kernel(in_ref, out_ref, grid_ref):
    for q in range(5):
        grid_ref[128 * q : 128 * q + 128, :] = in_ref[pl.ds(q, 128, stride=5), :].T
    for p in range(64):
        out_ref[:, 128 * p : 128 * p + 128] = grid_ref[pl.ds(p, 9, stride=64), :]


def tile_kernel(
    dev_ref, count_ref, recv_ref, list_ref, pg_ref, out_ref,
    rows, tri_lt, tri_gt, basis, found, expo, logs, prod, gw, spread, acc,
):
    tiles = list_ref.shape[0]
    for q in range(5):
        hi, mid, lo = split3(recv_ref[pl.ds(q, 128, stride=5), :].T)
        at = slice(128 * q, 128 * q + 128)
        rows[at, 0:128] = hi
        rows[at, 128:256] = mid
        rows[at, 256:384] = lo
    before = (iota((256, 256), 0) < iota((256, 256), 1)).astype(F32).astype(BF16)
    after = (iota((256, 256), 0) > iota((256, 256), 1)).astype(F32).astype(BF16)
    tri_lt[0:256] = before
    tri_lt[256:512] = before
    tri_gt[0:256] = after
    tri_gt[256:512] = after
    pix = iota((16, 256), 1)
    u = (pix % 16).astype(F32) - 7.5
    v = (pix // 16).astype(F32) - 7.5
    which = iota((16, 256), 0)
    moments = jnp.where(which == 0, 1.0, 0.0)
    moments = jnp.where(which == 1, u, moments)
    moments = jnp.where(which == 2, v, moments)
    moments = jnp.where(which == 3, u * u, moments)
    moments = jnp.where(which == 4, u * v, moments)
    moments = jnp.where(which == 5, v * v, moments)
    basis[...] = moments.astype(BF16)
    acc[...] = jnp.zeros_like(acc)
    first_tile = dev_ref[0] * tiles
    slot_row = iota((64, 256), 0)
    source_row = iota((128, 256), 0)

    def gather(s):
        t = s["t"]
        tile = first_tile + t
        s["ax"] = (tile % TILES_X * 16).astype(F32)
        s["ay"] = (tile // TILES_X % TILES_Y * 16).astype(F32)
        entry = list_ref[pl.ds(t, 1), :]
        s["entry"] = entry
        one = (source_row == entry // 64).astype(F32).astype(BF16)
        s["one"] = one
        found[s["k"]] = dot(rows[...], jnp.concatenate([one, one, one], axis=0))

    def pick(s):
        def field(f, mask):
            block = found[s["k"], 64 * f : 64 * f + 64, :]
            return jnp.sum(jnp.where(mask, block, 0.0), axis=0, keepdims=True)

        row_of = field(9, slot_row == s["entry"] % 64)
        mask = slot_row == row_of.astype(jnp.int32)
        s["mask"] = mask.astype(F32).astype(BF16)
        s["fields"] = [field(f, mask) for f in range(9)]

    def alphas(s):
        k = s["k"]
        cx, cy, a, b, c, _, _, _, opacity = s["fields"]
        side = iota((16, 256), 0).astype(F32) + 0.5
        dx = (s["ax"] + side) - cx
        dy = (s["ay"] + side) - cy
        live = iota((1, 256), 1) < count_ref[s["t"]]
        lead = jnp.where(live, jnp.log2(opacity), -100000.0)
        qa = (-0.5 * LOG2E) * a * dx * dx
        qb = -LOG2E * b * dx
        qc = (-0.5 * LOG2E) * c * dy * dy + lead
        for r in range(16):
            at = slice(16 * r, 16 * r + 16)
            e = qa + (qb * dy[r : r + 1, :] + qc[r : r + 1, :])
            alpha = jnp.exp2(e)
            kept = jnp.log2(1.0 - alpha)
            expo[k, at, :] = alpha
            prod[k, at, :] = jnp.exp2(e - kept)
            lhi, llo = split2(kept)
            logs[k, at, 0:256] = lhi
            logs[k, at, 256:512] = llo

    def weights(s):
        k = s["k"]
        chi, cmid, clo = split3(jnp.concatenate(s["fields"][5:8], axis=0))
        light = jnp.concatenate([pg_ref[ch, pl.ds(s["t"], 1), :] for ch in range(3)], axis=0)
        phi, pmid, plo = split3(light)
        zeros = jnp.zeros((14, 256), BF16)
        colors = jnp.concatenate([chi, cmid, clo, chi, cmid, chi, zeros], axis=0)
        lights = jnp.concatenate([phi, phi, phi, pmid, pmid, plo, zeros], axis=0)
        g = lax.dot_general(lights, colors, (((0,), (0,)), ((), ())), preferred_element_type=F32)
        lit = jnp.concatenate([phi, pmid, plo, jnp.zeros((7, 256), BF16)], axis=0)
        w = jnp.exp2(dot(logs[k], tri_lt[...])) * expo[k]
        whi, wlo = split2(w)
        rw = dot(lit, whi) + dot(lit, wlo)
        s["rw"] = rw[0:3] + rw[3:6] + rw[6:9]
        part = g * w
        expo[k] = part
        ghi, glo = split2(part)
        gw[k, :, 0:256] = ghi
        gw[k, :, 256:512] = glo

    def slopes(s):
        k = s["k"]
        h = expo[k] - dot(gw[k], tri_gt[...]) * prod[k]
        hhi, hlo = split2(h)
        s["rh"] = dot(basis[...], hhi) + dot(basis[...], hlo)

    def scatter(s):
        k = s["k"]
        cx, cy, a, b, c, _, _, _, opacity = s["fields"]
        rh, rw = s["rh"], s["rw"]
        n00, n10, n01, n20, n11, n02 = [rh[m : m + 1] for m in range(6)]
        cu = cx - (s["ax"] + 8.0)
        cv = cy - (s["ay"] + 8.0)
        m10 = n10 - cu * n00
        m01 = n01 - cv * n00
        m20 = n20 - cu * (n10 + m10)
        m11 = n11 - cu * n01 - cv * m10
        m02 = n02 - cv * (n01 + m01)
        grads = [
            a * m10 + b * m01,
            b * m10 + c * m01,
            -0.5 * m20,
            -m11,
            -0.5 * m02,
            rw[0:1],
            rw[1:2],
            rw[2:3],
            n00 / opacity,
        ]
        mask = s["mask"].reshape(4, 16, 256)
        for f in range(9):
            for piece, part in enumerate(split2(jnp.broadcast_to(grads[f], (16, 256)))):
                col = (2 * k + piece) * 256
                spread[64 * f : 64 * f + 64, col : col + 256] = (mask * part[None]).reshape(64, 256)

    def some_tiles(i, carry):
        states = [{"k": k, "t": i * UNROLL + k} for k in range(UNROLL)]
        for phase in (gather, pick, alphas, weights, slopes, scatter):
            for s in states:
                phase(s)
        ones = []
        for s in states:
            ones += [s["one"], s["one"]]
        acc[...] += lax.dot_general(
            spread[...],
            jnp.concatenate(ones, axis=1),
            (((1,), (1,)), ((), ())),
            preferred_element_type=F32,
        )
        return carry

    lax.fori_loop(0, tiles // UNROLL, some_tiles, 0)
    for q in range(5):
        out_ref[pl.ds(q, 128, stride=5), :] = acc[128 * q : 128 * q + 128, :].T


VMEM = pl.BlockSpec(memory_space=pltpu.VMEM)
SMEM = pl.BlockSpec(memory_space=pltpu.SMEM)


def pack(fields, rows, interpret=False):
    return pl.pallas_call(
        pack_kernel,
        out_shape=jax.ShapeDtypeStruct((640, 128), F32),
        in_specs=[VMEM, VMEM],
        out_specs=VMEM,
        scratch_shapes=[pltpu.VMEM((640, 128), F32)],
        name="pack",
        interpret=interpret,
    )(fields, rows)


def unpack(blocks, interpret=False):
    return pl.pallas_call(
        unpack_kernel,
        out_shape=jax.ShapeDtypeStruct((9, 8192), F32),
        in_specs=[VMEM],
        out_specs=VMEM,
        scratch_shapes=[pltpu.VMEM((640, 128), F32)],
        name="unpack",
        interpret=interpret,
    )(blocks)


def tile_work(device, tile_count, received, tile_list, light, interpret=False):
    return pl.pallas_call(
        tile_kernel,
        out_shape=jax.ShapeDtypeStruct((640, 128), F32),
        in_specs=[SMEM, SMEM, VMEM, VMEM, VMEM],
        out_specs=VMEM,
        scratch_shapes=[
            pltpu.VMEM((640, 384), BF16),
            pltpu.VMEM((512, 256), BF16),
            pltpu.VMEM((512, 256), BF16),
            pltpu.VMEM((16, 256), BF16),
            pltpu.VMEM((UNROLL, 640, 256), F32),
            pltpu.VMEM((UNROLL, 256, 256), F32),
            pltpu.VMEM((UNROLL, 256, 512), BF16),
            pltpu.VMEM((UNROLL, 256, 256), F32),
            pltpu.VMEM((UNROLL, 256, 512), BF16),
            pltpu.VMEM((640, 512 * UNROLL), BF16),
            pltpu.VMEM((640, 128), F32),
        ],
        name="splat_tiles",
        interpret=interpret,
    )(device, tile_count, received, tile_list, light)


def exchange(blocks):
    moved = lax.all_to_all(
        blocks.reshape(128, 1, 640), AXES, split_axis=0, concat_axis=0, tiled=True
    )
    return moved.reshape(640, 128)


def on_device(gauss_fields, send_rows, tile_list, tile_count, pixel_grad):
    received = exchange(pack(gauss_fields, send_rows[0].T))
    device = lax.axis_index(AXES).reshape(1).astype(jnp.int32)
    light = jnp.swapaxes(pixel_grad, 0, 1)
    grads = tile_work(device, tile_count, received, tile_list, light)
    return unpack(exchange(grads))


def solution(mesh):
    placed = (
        P(None, AXES),
        P(AXES, None, None),
        P(AXES, None),
        P(AXES),
        P(AXES, None, None),
    )
    return jax.shard_map(
        on_device, mesh=mesh, in_specs=placed, out_specs=P(None, AXES), check_vma=False
    )
```

```python
import jax
import jax.numpy as jnp
from jax import lax
from jax.experimental import pallas as pl
from jax.experimental.pallas import tpu as pltpu
from jax.sharding import PartitionSpec as P

AXES = ("gauss", "pix")
TILES_X = 32
TILES_Y = 8
LOG2E = 1.4426950408889634
F32 = jnp.float32
BF16 = jnp.bfloat16
TOGETHER = 2


def split2(x):
    hi = x.astype(BF16)
    return hi, (x - hi.astype(F32)).astype(BF16)


def split3(x):
    hi = x.astype(BF16)
    rest = x - hi.astype(F32)
    mid = rest.astype(BF16)
    return hi, mid, (rest - mid.astype(F32)).astype(BF16)


def dot(a, b):
    return jnp.dot(a, b, preferred_element_type=F32)


def iota(shape, dim):
    return lax.broadcasted_iota(jnp.int32, shape, dim)


def pack_kernel(fields_ref, rows_ref, out_ref, grid_ref):
    for p in range(64):
        grid_ref[pl.ds(p, 9, stride=64), :] = fields_ref[:, 128 * p : 128 * p + 128]
    grid_ref[576:640, :] = jnp.zeros((64, 128), F32)
    row = rows_ref[...] // 128
    order = jnp.concatenate([row, row + 64], axis=0).T
    for q in range(5):
        block = grid_ref[128 * q : 128 * q + 128, :].T
        out_ref[pl.ds(q, 128, stride=5), :] = jnp.take_along_axis(block, order, axis=1)


def invert_kernel(rows_ref, out_ref):
    row = rows_ref[...] // 128
    place = iota((64, 128), 0)
    slot = jnp.zeros((64, 128), jnp.int32)
    for j in range(64):
        slot = jnp.where(row[j : j + 1, :] == place, j, slot)
    out_ref[...] = jnp.concatenate([slot, slot + 64], axis=0).T


def unpack_kernel(in_ref, slot_ref, out_ref, grid_ref):
    order = slot_ref[...]
    for q in range(5):
        block = jnp.take_along_axis(in_ref[pl.ds(q, 128, stride=5), :], order, axis=1)
        grid_ref[128 * q : 128 * q + 128, :] = block.T
    for p in range(64):
        out_ref[:, 128 * p : 128 * p + 128] = grid_ref[pl.ds(p, 9, stride=64), :]


def tile_kernel(
    dev_ref, count_ref, recv_ref, list_ref, pg_ref, out_ref,
    turned, rows, rows_lo, tri_lt, tri_gt, found, expo, logs, prod, part, gw, wts, spread, acc,
):
    tiles = list_ref.shape[0]
    for q in range(5):
        turned[128 * q : 128 * q + 128, :] = recv_ref[pl.ds(q, 128, stride=5), :].T
    for f in range(9):
        for half in range(2):
            at = slice(32 * f, 32 * f + 32)
            lane = 128 * half
            pieces = split3(turned[64 * f + 32 * half : 64 * f + 32 * half + 32, :])
            rows[at, lane : lane + 128] = pieces[0]
            rows[at, 256 + lane : 384 + lane] = pieces[1]
            if f < 2:
                rows_lo[at, lane : lane + 128] = pieces[2]
    before = (iota((256, 256), 0) < iota((256, 256), 1)).astype(F32).astype(BF16)
    after = (iota((256, 256), 0) > iota((256, 256), 1)).astype(F32).astype(BF16)
    tri_lt[0:256] = before
    tri_lt[256:512] = before
    tri_gt[0:256] = after
    tri_gt[256:512] = after
    acc[...] = jnp.zeros_like(acc)
    first_tile = dev_ref[0] * tiles

    def gather(s):
        t = s["t"]
        tile = first_tile + t
        s["ax"] = (tile % TILES_X * 16).astype(F32)
        s["ay"] = (tile // TILES_X % TILES_Y * 16).astype(F32)
        entry = list_ref[pl.ds(t, 1), :]
        key = (entry // 32) % 2 * 128 + entry // 64
        s["one"] = (iota((256, 256), 0) == key).astype(F32).astype(BF16)
        s["mask"] = iota((32, 256), 0) == entry % 32
        found[s["b"], 0:288] = dot(rows[...], jnp.concatenate([s["one"], s["one"]], axis=0))
        found[s["b"], 288:352] = dot(rows_lo[...], s["one"])

    def pick(s):
        def field(f):
            block = jnp.where(s["mask"], found[s["b"], 32 * f : 32 * f + 32, :], 0.0)
            return jnp.sum(block, axis=0, keepdims=True)

        s["fields"] = [field(f) for f in range(9)]
        s["fields"][0] += field(9)
        s["fields"][1] += field(10)

    def alphas(s):
        b, k = s["b"], s["k"]
        cx, cy, a, b_, c, _, _, _, opacity = s["fields"]
        side = iota((16, 256), 0).astype(F32) + 0.5
        dx = (s["ax"] + side) - cx
        dy = (s["ay"] + side) - cy
        live = iota((1, 256), 1) < count_ref[s["t"]]
        lead = jnp.where(live, jnp.log2(opacity), -100000.0)
        qa = (-0.5 * LOG2E) * a * dx * dx
        qb = -LOG2E * b_ * dx
        qc = (-0.5 * LOG2E) * c * dy * dy + lead
        for r in range(16):
            at = slice(16 * r, 16 * r + 16)
            e = qa + (qb * dy[r : r + 1, :] + qc[r : r + 1, :])
            alpha = jnp.exp2(e)
            kept = jnp.log2(1.0 - alpha)
            expo[b, at, :] = alpha
            prod[b, at, :] = jnp.exp2(e - kept)
            lhi, llo = split2(kept)
            row = 256 * k + 16 * r
            logs[s["g"], row : row + 16, 0:256] = lhi
            logs[s["g"], row : row + 16, 256:512] = llo

    def weights(s, cum):
        b, k = s["b"], s["k"]
        chi, cmid = split2(jnp.concatenate(s["fields"][5:8], axis=0))
        light = jnp.concatenate([pg_ref[ch, pl.ds(s["t"], 1), :] for ch in range(3)], axis=0)
        phi, pmid, plo = split3(light)
        zero = jnp.zeros((1, 256), BF16)
        colors = jnp.concatenate([chi, cmid, chi, cmid, chi, zero], axis=0)
        lights = jnp.concatenate([phi, phi, pmid, pmid, plo, zero], axis=0)
        g = lax.dot_general(lights, colors, (((0,), (0,)), ((), ())), preferred_element_type=F32)
        s["lit"] = jnp.concatenate([phi, pmid, plo, jnp.zeros((7, 256), BF16)], axis=0)
        for r in range(16):
            at = slice(16 * r, 16 * r + 16)
            w = jnp.exp2(cum[256 * k + 16 * r : 256 * k + 16 * r + 16]) * expo[b, at, :]
            whi, wlo = split2(w)
            wts[b, at, :] = whi
            wts[b, 256 + 16 * r : 272 + 16 * r, :] = wlo
            gpart = g[at] * w
            part[b, at, :] = gpart
            ghi, glo = split2(gpart)
            row = 256 * k + 16 * r
            gw[s["g"], row : row + 16, 0:256] = ghi
            gw[s["g"], row : row + 16, 256:512] = glo

    def slopes(s, behind):
        b, k = s["b"], s["k"]
        rw = dot(jnp.concatenate([s["lit"], s["lit"]], axis=1), wts[b])
        s["rw"] = rw[0:3] + rw[3:6] + rw[6:9]
        once = jnp.zeros((16, 256), F32)
        twice = jnp.zeros((16, 256), F32)
        thrice = jnp.zeros((16, 256), F32)
        for r in range(16):
            at = slice(16 * r, 16 * r + 16)
            row = 256 * k + 16 * r
            h = part[b, at, :] - behind[row : row + 16] * prod[b, at, :]
            once = once + h
            twice = twice + once
            thrice = thrice + twice
        h0 = once
        h1 = 8.5 * once - twice
        h2 = 2.0 * thrice - 18.0 * twice + 72.25 * once
        u = iota((16, 1), 0).astype(F32) - 7.5

        def over(x):
            return jnp.sum(x, axis=0, keepdims=True)

        s["n"] = [over(h0), over(u * h0), over(h1), over(u * u * h0), over(u * h1), over(h2)]

    def scatter(s):
        cx, cy, a, b, c, _, _, _, opacity = s["fields"]
        rw = s["rw"]
        n00, n10, n01, n20, n11, n02 = s["n"]
        cu = cx - (s["ax"] + 8.0)
        cv = cy - (s["ay"] + 8.0)
        m10 = n10 - cu * n00
        m01 = n01 - cv * n00
        m20 = n20 - cu * (n10 + m10)
        m11 = n11 - cu * n01 - cv * m10
        m02 = n02 - cv * (n01 + m01)
        grads = [
            a * m10 + b * m01,
            b * m10 + c * m01,
            -0.5 * m20,
            -m11,
            -0.5 * m02,
            rw[0:1],
            rw[1:2],
            rw[2:3],
            n00 / opacity,
        ]
        mask = s["mask"].astype(F32).astype(BF16).reshape(2, 16, 256)
        for f in range(9):
            for piece, val in enumerate(split2(jnp.broadcast_to(grads[f], (16, 256)))):
                col = (2 * s["k"] + piece) * 256
                spread[s["g"], 32 * f : 32 * f + 32, col : col + 256] = (
                    mask * val[None]
                ).reshape(32, 256)

    def front(i):
        states = [
            {"b": TOGETHER * (i % 2) + k, "k": k, "g": i % 2, "t": i * TOGETHER + k}
            for k in range(TOGETHER)
        ]
        for s in states:
            gather(s)
        for s in states:
            pick(s)
            alphas(s)
        return states

    def back(states):
        slot = states[0]["g"]
        cum = dot(logs[slot], tri_lt[...])
        for s in states:
            weights(s, cum)
        behind = dot(gw[slot], tri_gt[...])
        for s in states:
            slopes(s, behind)
            scatter(s)
        ones = []
        for s in states:
            ones += [s["one"], s["one"]]
        acc[...] += lax.dot_general(
            spread[slot],
            jnp.concatenate(ones, axis=1),
            (((1,), (1,)), ((), ())),
            preferred_element_type=F32,
        )

    steps = tiles // TOGETHER
    ready = front(0)
    for i in range(steps):
        following = front(i + 1) if i + 1 < steps else None
        back(ready)
        ready = following
    for f in range(9):
        for half in range(2):
            at = 64 * f + 32 * half
            turned[at : at + 32, :] = acc[32 * f : 32 * f + 32, 128 * half : 128 * half + 128]
    for q in range(5):
        out_ref[pl.ds(q, 128, stride=5), :] = turned[128 * q : 128 * q + 128, :].T


VMEM = pl.BlockSpec(memory_space=pltpu.VMEM)
SMEM = pl.BlockSpec(memory_space=pltpu.SMEM)
ON_CHIP = True


def held(x, interpret):
    if interpret or not ON_CHIP:
        return x
    return pltpu.with_memory_space_constraint(x, pltpu.VMEM)


def block_shape(interpret):
    if interpret or not ON_CHIP:
        return jax.ShapeDtypeStruct((640, 128), F32)
    return pltpu.VMEM((640, 128), F32)


def pack(fields, rows, interpret=False):
    return pl.pallas_call(
        pack_kernel,
        out_shape=block_shape(interpret),
        in_specs=[VMEM, VMEM],
        out_specs=VMEM,
        scratch_shapes=[pltpu.VMEM((640, 128), F32)],
        name="pack",
        interpret=interpret,
    )(fields, rows)


def invert(rows, interpret=False):
    return pl.pallas_call(
        invert_kernel,
        out_shape=jax.ShapeDtypeStruct((128, 128), jnp.int32),
        in_specs=[VMEM],
        out_specs=VMEM,
        name="invert",
        interpret=interpret,
    )(rows)


def unpack(blocks, slots, interpret=False):
    return pl.pallas_call(
        unpack_kernel,
        out_shape=jax.ShapeDtypeStruct((9, 8192), F32),
        in_specs=[VMEM, VMEM],
        out_specs=VMEM,
        scratch_shapes=[pltpu.VMEM((640, 128), F32)],
        name="unpack",
        interpret=interpret,
    )(held(blocks, interpret), slots)


def tile_work(device, tile_count, received, tile_list, light, interpret=False):
    both = 2 * TOGETHER
    return pl.pallas_call(
        tile_kernel,
        out_shape=block_shape(interpret),
        in_specs=[SMEM, SMEM, VMEM, VMEM, VMEM],
        out_specs=VMEM,
        scratch_shapes=[
            pltpu.VMEM((640, 128), F32),
            pltpu.VMEM((288, 512), BF16),
            pltpu.VMEM((64, 256), BF16),
            pltpu.VMEM((512, 256), BF16),
            pltpu.VMEM((512, 256), BF16),
            pltpu.VMEM((both, 352, 256), F32),
            pltpu.VMEM((both, 256, 256), F32),
            pltpu.VMEM((2, 256 * TOGETHER, 512), BF16),
            pltpu.VMEM((both, 256, 256), F32),
            pltpu.VMEM((both, 256, 256), F32),
            pltpu.VMEM((2, 256 * TOGETHER, 512), BF16),
            pltpu.VMEM((both, 512, 256), BF16),
            pltpu.VMEM((2, 288, 512 * TOGETHER), BF16),
            pltpu.VMEM((288, 256), F32),
        ],
        name="splat_tiles",
        interpret=interpret,
    )(device, tile_count, held(received, interpret), tile_list, light)


def exchange(blocks):
    moved = lax.all_to_all(
        blocks.reshape(128, 1, 640), AXES, split_axis=0, concat_axis=0, tiled=True
    )
    return moved.reshape(640, 128)


def on_device(gauss_fields, send_rows, tile_list, tile_count, pixel_grad):
    slot_rows = send_rows[0].T
    received = exchange(pack(gauss_fields, slot_rows))
    device = lax.axis_index(AXES).reshape(1).astype(jnp.int32)
    light = jnp.swapaxes(pixel_grad, 0, 1)
    grads = tile_work(device, tile_count, received, tile_list, light)
    return unpack(exchange(grads), invert(slot_rows))


def solution(mesh):
    placed = (
        P(None, AXES),
        P(AXES, None, None),
        P(AXES, None),
        P(AXES),
        P(AXES, None, None),
    )
    return jax.shard_map(
        on_device, mesh=mesh, in_specs=placed, out_specs=P(None, AXES), check_vma=False
    )
```

```python
import jax
import jax.numpy as jnp
from jax import lax
from jax.experimental import pallas as pl
from jax.experimental.pallas import tpu as pltpu
from jax.sharding import PartitionSpec as P

AXES = ("gauss", "pix")
TILES_X = 32
TILES_Y = 8
LOG2E = 1.4426950408889634
F32 = jnp.float32
BF16 = jnp.bfloat16
TOGETHER = 2


def split2(x):
    hi = x.astype(BF16)
    return hi, (x - hi.astype(F32)).astype(BF16)


def split3(x):
    hi = x.astype(BF16)
    rest = x - hi.astype(F32)
    mid = rest.astype(BF16)
    return hi, mid, (rest - mid.astype(F32)).astype(BF16)


def dot(a, b):
    return jnp.dot(a, b, preferred_element_type=F32)


def iota(shape, dim):
    return lax.broadcasted_iota(jnp.int32, shape, dim)


def pack_kernel(fields_ref, rows_ref, out_ref, slot_ref, grid_ref):
    for p in range(64):
        grid_ref[pl.ds(p, 9, stride=64), :] = fields_ref[:, 128 * p : 128 * p + 128]
    grid_ref[576:640, :] = jnp.zeros((64, 128), F32)
    row = rows_ref[...] // 128
    order = jnp.concatenate([row, row + 64], axis=0).T
    for q in range(5):
        block = grid_ref[128 * q : 128 * q + 128, :].T
        out_ref[pl.ds(q, 128, stride=5), :] = jnp.take_along_axis(block, order, axis=1)
    place = iota((64, 128), 0)
    slot = jnp.zeros((64, 128), jnp.int32)
    for j in range(64):
        slot = jnp.where(row[j : j + 1, :] == place, j, slot)
    slot_ref[...] = jnp.concatenate([slot, slot + 64], axis=0).T


def unpack_kernel(in_ref, slot_ref, out_ref, grid_ref):
    order = slot_ref[...]
    for q in range(5):
        block = jnp.take_along_axis(in_ref[pl.ds(q, 128, stride=5), :], order, axis=1)
        grid_ref[128 * q : 128 * q + 128, :] = block.T
    for p in range(64):
        out_ref[:, 128 * p : 128 * p + 128] = grid_ref[pl.ds(p, 9, stride=64), :]


def tile_kernel(
    dev_ref, count_ref, recv_ref, list_ref, pg_ref, out_ref,
    turned, rows, rows_lo, tri_lt, tri_gt, found, expo, logs, prod, part, gw, wts, spread, acc,
):
    tiles = list_ref.shape[0]
    for q in range(5):
        turned[128 * q : 128 * q + 128, :] = recv_ref[pl.ds(q, 128, stride=5), :].T
    for f in range(9):
        for half in range(2):
            at = slice(32 * f, 32 * f + 32)
            lane = 128 * half
            pieces = split3(turned[64 * f + 32 * half : 64 * f + 32 * half + 32, :])
            rows[at, lane : lane + 128] = pieces[0]
            rows[at, 256 + lane : 384 + lane] = pieces[1]
            if f < 2:
                rows_lo[at, lane : lane + 128] = pieces[2]
    before = (iota((256, 256), 0) < iota((256, 256), 1)).astype(F32).astype(BF16)
    after = (iota((256, 256), 0) > iota((256, 256), 1)).astype(F32).astype(BF16)
    tri_lt[0:256] = before
    tri_lt[256:512] = before
    tri_gt[0:256] = after
    tri_gt[256:512] = after
    acc[...] = jnp.zeros_like(acc)
    first_tile = dev_ref[0] * tiles

    def gather(s):
        t = s["t"]
        tile = first_tile + t
        s["ax"] = (tile % TILES_X * 16).astype(F32)
        s["ay"] = (tile // TILES_X % TILES_Y * 16).astype(F32)
        entry = list_ref[pl.ds(t, 1), :]
        key = (entry // 32) % 2 * 128 + entry // 64
        s["one"] = (iota((256, 256), 0) == key).astype(F32).astype(BF16)
        s["mask"] = iota((32, 256), 0) == entry % 32
        found[s["b"], 0:288] = dot(rows[...], jnp.concatenate([s["one"], s["one"]], axis=0))
        found[s["b"], 288:352] = dot(rows_lo[...], s["one"])

    def pick(s):
        def field(f):
            block = jnp.where(s["mask"], found[s["b"], 32 * f : 32 * f + 32, :], 0.0)
            return jnp.sum(block, axis=0, keepdims=True)

        s["fields"] = [field(f) for f in range(9)]
        s["fields"][0] += field(9)
        s["fields"][1] += field(10)

    def alphas(s):
        b, k = s["b"], s["k"]
        cx, cy, a, b_, c, _, _, _, opacity = s["fields"]
        side = iota((16, 256), 0).astype(F32) + 0.5
        dx = (s["ax"] + side) - cx
        dy = (s["ay"] + side) - cy
        live = iota((1, 256), 1) < count_ref[s["t"]]
        lead = jnp.where(live, jnp.log2(opacity), -100000.0)
        qa = (-0.5 * LOG2E) * a * dx * dx
        qb = -LOG2E * b_ * dx
        qc = (-0.5 * LOG2E) * c * dy * dy + lead
        for r in range(16):
            at = slice(16 * r, 16 * r + 16)
            e = qa + (qb * dy[r : r + 1, :] + qc[r : r + 1, :])
            alpha = jnp.exp2(e)
            kept = jnp.log2(1.0 - alpha)
            expo[b, at, :] = alpha
            prod[b, at, :] = jnp.exp2(e - kept)
            lhi, llo = split2(kept)
            row = 256 * k + 16 * r
            logs[s["g"], row : row + 16, 0:256] = lhi
            logs[s["g"], row : row + 16, 256:512] = llo

    def weights(s, cum):
        b, k = s["b"], s["k"]
        chi, cmid = split2(jnp.concatenate(s["fields"][5:8], axis=0))
        light = jnp.concatenate([pg_ref[ch, pl.ds(s["t"], 1), :] for ch in range(3)], axis=0)
        phi, pmid, plo = split3(light)
        zero = jnp.zeros((1, 256), BF16)
        colors = jnp.concatenate([chi, cmid, chi, cmid, chi, zero], axis=0)
        lights = jnp.concatenate([phi, phi, pmid, pmid, plo, zero], axis=0)
        g = lax.dot_general(lights, colors, (((0,), (0,)), ((), ())), preferred_element_type=F32)
        s["lit"] = jnp.concatenate([phi, pmid, plo, jnp.zeros((7, 256), BF16)], axis=0)
        for r in range(16):
            at = slice(16 * r, 16 * r + 16)
            w = jnp.exp2(cum[256 * k + 16 * r : 256 * k + 16 * r + 16]) * expo[b, at, :]
            whi, wlo = split2(w)
            wts[b, at, :] = whi
            wts[b, 256 + 16 * r : 272 + 16 * r, :] = wlo
            gpart = g[at] * w
            part[b, at, :] = gpart
            ghi, glo = split2(gpart)
            row = 256 * k + 16 * r
            gw[s["g"], row : row + 16, 0:256] = ghi
            gw[s["g"], row : row + 16, 256:512] = glo

    def slopes(s, behind):
        b, k = s["b"], s["k"]
        rw = dot(jnp.concatenate([s["lit"], s["lit"]], axis=1), wts[b])
        s["rw"] = rw[0:3] + rw[3:6] + rw[6:9]
        once = jnp.zeros((16, 256), F32)
        twice = jnp.zeros((16, 256), F32)
        thrice = jnp.zeros((16, 256), F32)
        for r in range(16):
            at = slice(16 * r, 16 * r + 16)
            row = 256 * k + 16 * r
            h = part[b, at, :] - behind[row : row + 16] * prod[b, at, :]
            once = once + h
            twice = twice + once
            thrice = thrice + twice
        h0 = once
        h1 = 8.5 * once - twice
        h2 = 2.0 * thrice - 18.0 * twice + 72.25 * once
        u = iota((16, 1), 0).astype(F32) - 7.5

        def over(x):
            return jnp.sum(x, axis=0, keepdims=True)

        s["n"] = [over(h0), over(u * h0), over(h1), over(u * u * h0), over(u * h1), over(h2)]

    def scatter(s):
        cx, cy, a, b, c, _, _, _, opacity = s["fields"]
        rw = s["rw"]
        n00, n10, n01, n20, n11, n02 = s["n"]
        cu = cx - (s["ax"] + 8.0)
        cv = cy - (s["ay"] + 8.0)
        m10 = n10 - cu * n00
        m01 = n01 - cv * n00
        m20 = n20 - cu * (n10 + m10)
        m11 = n11 - cu * n01 - cv * m10
        m02 = n02 - cv * (n01 + m01)
        grads = [
            a * m10 + b * m01,
            b * m10 + c * m01,
            -0.5 * m20,
            -m11,
            -0.5 * m02,
            rw[0:1],
            rw[1:2],
            rw[2:3],
            n00 / opacity,
        ]
        mask = s["mask"].astype(F32).astype(BF16).reshape(2, 16, 256)
        for f in range(9):
            for piece, val in enumerate(split2(jnp.broadcast_to(grads[f], (16, 256)))):
                col = (2 * s["k"] + piece) * 256
                spread[s["g"], 32 * f : 32 * f + 32, col : col + 256] = (
                    mask * val[None]
                ).reshape(32, 256)

    def front(i):
        states = [
            {"b": TOGETHER * (i % 2) + k, "k": k, "g": i % 2, "t": i * TOGETHER + k}
            for k in range(TOGETHER)
        ]
        for s in states:
            gather(s)
        for s in states:
            pick(s)
            alphas(s)
        return states

    def back(states):
        slot = states[0]["g"]
        cum = dot(logs[slot], tri_lt[...])
        for s in states:
            weights(s, cum)
        behind = dot(gw[slot], tri_gt[...])
        for s in states:
            slopes(s, behind)
            scatter(s)
        ones = []
        for s in states:
            ones += [s["one"], s["one"]]
        acc[...] += lax.dot_general(
            spread[slot],
            jnp.concatenate(ones, axis=1),
            (((1,), (1,)), ((), ())),
            preferred_element_type=F32,
        )

    steps = tiles // TOGETHER
    ready = front(0)
    for i in range(steps):
        following = front(i + 1) if i + 1 < steps else None
        back(ready)
        ready = following
    for f in range(9):
        for half in range(2):
            at = 64 * f + 32 * half
            turned[at : at + 32, :] = acc[32 * f : 32 * f + 32, 128 * half : 128 * half + 128]
    for q in range(5):
        out_ref[pl.ds(q, 128, stride=5), :] = turned[128 * q : 128 * q + 128, :].T


VMEM = pl.BlockSpec(memory_space=pltpu.VMEM)
SMEM = pl.BlockSpec(memory_space=pltpu.SMEM)
ON_CHIP = True


def held(x, interpret):
    if interpret or not ON_CHIP:
        return x
    return pltpu.with_memory_space_constraint(x, pltpu.VMEM)


def on_chip(shape, dtype, interpret):
    if interpret or not ON_CHIP:
        return jax.ShapeDtypeStruct(shape, dtype)
    return pltpu.VMEM(shape, dtype)


def block_shape(interpret):
    return on_chip((640, 128), F32, interpret)


def pack(fields, rows, interpret=False):
    return pl.pallas_call(
        pack_kernel,
        out_shape=[block_shape(interpret), on_chip((128, 128), jnp.int32, interpret)],
        in_specs=[VMEM, VMEM],
        out_specs=[VMEM, VMEM],
        scratch_shapes=[pltpu.VMEM((640, 128), F32)],
        name="pack",
        interpret=interpret,
    )(fields, rows)


def unpack(blocks, slots, interpret=False):
    return pl.pallas_call(
        unpack_kernel,
        out_shape=jax.ShapeDtypeStruct((9, 8192), F32),
        in_specs=[VMEM, VMEM],
        out_specs=VMEM,
        scratch_shapes=[pltpu.VMEM((640, 128), F32)],
        name="unpack",
        interpret=interpret,
    )(held(blocks, interpret), held(slots, interpret))


def tile_work(device, tile_count, received, tile_list, light, interpret=False):
    both = 2 * TOGETHER
    return pl.pallas_call(
        tile_kernel,
        out_shape=block_shape(interpret),
        in_specs=[SMEM, SMEM, VMEM, VMEM, VMEM],
        out_specs=VMEM,
        scratch_shapes=[
            pltpu.VMEM((640, 128), F32),
            pltpu.VMEM((288, 512), BF16),
            pltpu.VMEM((64, 256), BF16),
            pltpu.VMEM((512, 256), BF16),
            pltpu.VMEM((512, 256), BF16),
            pltpu.VMEM((both, 352, 256), F32),
            pltpu.VMEM((both, 256, 256), F32),
            pltpu.VMEM((2, 256 * TOGETHER, 512), BF16),
            pltpu.VMEM((both, 256, 256), F32),
            pltpu.VMEM((both, 256, 256), F32),
            pltpu.VMEM((2, 256 * TOGETHER, 512), BF16),
            pltpu.VMEM((both, 512, 256), BF16),
            pltpu.VMEM((2, 288, 512 * TOGETHER), BF16),
            pltpu.VMEM((288, 256), F32),
        ],
        name="splat_tiles",
        interpret=interpret,
    )(device, tile_count, held(received, interpret), tile_list, light)


def exchange(blocks):
    moved = lax.all_to_all(
        blocks.reshape(128, 1, 640), AXES, split_axis=0, concat_axis=0, tiled=True
    )
    return moved.reshape(640, 128)


def on_device(gauss_fields, send_rows, tile_list, tile_count, pixel_grad):
    device = lax.axis_index(AXES).reshape(1).astype(jnp.int32)
    gauss_fields, device = lax.optimization_barrier((gauss_fields, device))
    blocks, slots = pack(gauss_fields, send_rows[0].T)
    received = exchange(blocks)
    light = jnp.swapaxes(pixel_grad, 0, 1)
    grads = tile_work(device, tile_count, received, tile_list, light)
    return unpack(exchange(grads), slots)


def solution(mesh):
    placed = (
        P(None, AXES),
        P(AXES, None, None),
        P(AXES, None),
        P(AXES),
        P(AXES, None, None),
    )
    return jax.shard_map(
        on_device, mesh=mesh, in_specs=placed, out_specs=P(None, AXES), check_vma=False
    )
```

```python
import jax
import jax.numpy as jnp
from jax import lax
from jax.experimental import pallas as pl
from jax.experimental.pallas import tpu as pltpu
from jax.sharding import PartitionSpec as P

AXES = ("gauss", "pix")
TILES_X = 32
TILES_Y = 8
LOG2E = 1.4426950408889634
F32 = jnp.float32
BF16 = jnp.bfloat16
TOGETHER = 2


def split2(x):
    hi = x.astype(BF16)
    return hi, (x - hi.astype(F32)).astype(BF16)


def split3(x):
    hi = x.astype(BF16)
    rest = x - hi.astype(F32)
    mid = rest.astype(BF16)
    return hi, mid, (rest - mid.astype(F32)).astype(BF16)


def dot(a, b):
    return jnp.dot(a, b, preferred_element_type=F32)


def iota(shape, dim):
    return lax.broadcasted_iota(jnp.int32, shape, dim)


def pack_kernel(
    dev_ref, count_ref, fields_ref, rows_ref, list_ref, pg_ref,
    out_ref, slot_ref, list_out, pg_out, tile_out, grid_ref,
):
    list_out[...] = list_ref[...]
    pg_out[...] = pg_ref[...]
    tiles = list_ref.shape[0]
    for t in range(tiles):
        tile = dev_ref[0] * tiles + t
        live = iota((1, 256), 1) < count_ref[t]
        tile_out[t : t + 1, :] = jnp.where(live, 0.0, -100000.0)
        anchor_x = (tile % TILES_X * 16).astype(F32)
        anchor_y = (tile // TILES_X % TILES_Y * 16).astype(F32)
        tile_out[tiles + t : tiles + t + 1, :] = jnp.full((1, 256), anchor_x, F32)
        tile_out[2 * tiles + t : 2 * tiles + t + 1, :] = jnp.full((1, 256), anchor_y, F32)
    for p in range(64):
        grid_ref[pl.ds(p, 9, stride=64), :] = fields_ref[:, 128 * p : 128 * p + 128]
    grid_ref[576:640, :] = jnp.zeros((64, 128), F32)
    row = rows_ref[...] // 128
    order = jnp.concatenate([row, row + 64], axis=0).T
    for q in range(5):
        block = grid_ref[128 * q : 128 * q + 128, :].T
        out_ref[pl.ds(q, 128, stride=5), :] = jnp.take_along_axis(block, order, axis=1)
    place = iota((64, 128), 0)
    slot = jnp.zeros((64, 128), jnp.int32)
    for j in range(64):
        slot = jnp.where(row[j : j + 1, :] == place, j, slot)
    slot_ref[...] = jnp.concatenate([slot, slot + 64], axis=0).T


def unpack_kernel(in_ref, slot_ref, out_ref, grid_ref):
    order = slot_ref[...]
    for q in range(5):
        block = jnp.take_along_axis(in_ref[pl.ds(q, 128, stride=5), :], order, axis=1)
        grid_ref[128 * q : 128 * q + 128, :] = block.T
    for p in range(64):
        out_ref[:, 128 * p : 128 * p + 128] = grid_ref[pl.ds(p, 9, stride=64), :]


def tile_kernel(
    recv_ref, list_ref, pg_ref, tile_ref, out_ref,
    turned, rows, rows_lo, tri_le, tri_gt, found, logs, odds, part, gw, wts, spread, acc, place,
):
    tiles = list_ref.shape[0]
    for q in range(5):
        turned[128 * q : 128 * q + 128, :] = recv_ref[pl.ds(q, 128, stride=5), :].T
    for f in range(9):
        for half in range(2):
            at = slice(32 * f, 32 * f + 32)
            lane = 128 * half
            pieces = split3(turned[64 * f + 32 * half : 64 * f + 32 * half + 32, :])
            rows[at, lane : lane + 128] = pieces[0]
            rows[at, 256 + lane : 384 + lane] = pieces[1]
            if f < 2:
                rows_lo[at, lane : lane + 128] = pieces[2]
    before = (iota((256, 256), 0) <= iota((256, 256), 1)).astype(F32).astype(BF16)
    after = (iota((256, 256), 0) > iota((256, 256), 1)).astype(F32).astype(BF16)
    tri_le[0:256] = before
    tri_le[256:512] = before
    tri_gt[0:256] = after
    tri_gt[256:512] = after
    acc[...] = jnp.zeros_like(acc)
    place[...] = iota((256, 256), 0).astype(F32).astype(BF16)

    def gather(s):
        t = s["t"]
        s["ax"] = tile_ref[tiles + t : tiles + t + 1, :]
        s["ay"] = tile_ref[2 * tiles + t : 2 * tiles + t + 1, :]
        entry = list_ref[t : t + 1, :]
        key = (entry // 32) % 2 * 128 + entry // 64
        keys = jnp.broadcast_to(key.astype(F32), (16, 256)).astype(BF16)
        hit = place[...].reshape(16, 16, 256) == keys[None]
        s["one"] = jnp.where(hit, jnp.ones((), BF16), jnp.zeros((), BF16)).reshape(256, 256)
        s["mask"] = (iota((32, 256), 0) == entry % 32).astype(F32)
        found[s["b"], 0:288] = dot(rows[...], jnp.concatenate([s["one"], s["one"]], axis=0))
        found[s["b"], 288:352] = dot(rows_lo[...], s["one"])

    def pick(s):
        def field(f):
            block = s["mask"] * found[s["b"], 32 * f : 32 * f + 32, :]
            return jnp.sum(block, axis=0, keepdims=True)

        s["fields"] = [field(f) for f in range(9)]
        s["fields"][0] += field(9)
        s["fields"][1] += field(10)

    def alphas(s):
        b, k = s["b"], s["k"]
        cx, cy, a, b_, c, _, _, _, opacity = s["fields"]
        side = iota((16, 256), 0).astype(F32) + 0.5
        dx = (s["ax"] + side) - cx
        dy = (s["ay"] + side) - cy
        lead = jnp.log2(opacity) + tile_ref[s["t"] : s["t"] + 1, :]
        qa = (-0.5 * LOG2E) * a * dx * dx
        qb = -LOG2E * b_ * dx
        qc = (-0.5 * LOG2E) * c * dy * dy + lead
        for r in range(16):
            at = slice(16 * r, 16 * r + 16)
            e = qa + (qb * dy[r : r + 1, :] + qc[r : r + 1, :])
            alpha = jnp.exp2(e)
            kept = jnp.log2(1.0 - alpha)
            odds[b, at, :] = jnp.exp2(e - kept)
            lhi, llo = split2(kept)
            row = 256 * k + 16 * r
            logs[s["g"], row : row + 16, 0:256] = lhi
            logs[s["g"], row : row + 16, 256:512] = llo

    def weights(s, cum):
        b, k = s["b"], s["k"]
        chi, cmid = split2(jnp.concatenate(s["fields"][5:8], axis=0))
        light = jnp.concatenate([pg_ref[ch, s["t"] : s["t"] + 1, :] for ch in range(3)], axis=0)
        phi, pmid, plo = split3(light)
        zero = jnp.zeros((1, 256), BF16)
        colors = jnp.concatenate([chi, cmid, chi, cmid, chi, zero], axis=0)
        lights = jnp.concatenate([phi, phi, pmid, pmid, plo, zero], axis=0)
        g = lax.dot_general(lights, colors, (((0,), (0,)), ((), ())), preferred_element_type=F32)
        s["lit"] = jnp.concatenate([phi, pmid, plo, jnp.zeros((7, 256), BF16)], axis=0)
        for r in range(16):
            at = slice(16 * r, 16 * r + 16)
            w = jnp.exp2(cum[256 * k + 16 * r : 256 * k + 16 * r + 16]) * odds[b, at, :]
            whi, wlo = split2(w)
            wts[b, at, :] = whi
            wts[b, 256 + 16 * r : 272 + 16 * r, :] = wlo
            gpart = g[at] * w
            part[b, at, :] = gpart
            ghi, glo = split2(gpart)
            row = 256 * k + 16 * r
            gw[s["g"], row : row + 16, 0:256] = ghi
            gw[s["g"], row : row + 16, 256:512] = glo

    def slopes(s, behind):
        b, k = s["b"], s["k"]
        rw = dot(jnp.concatenate([s["lit"], s["lit"]], axis=1), wts[b])
        s["rw"] = rw[0:3] + rw[3:6] + rw[6:9]
        once = jnp.zeros((16, 256), F32)
        twice = jnp.zeros((16, 256), F32)
        thrice = jnp.zeros((16, 256), F32)
        for r in range(16):
            at = slice(16 * r, 16 * r + 16)
            row = 256 * k + 16 * r
            h = part[b, at, :] - behind[row : row + 16] * odds[b, at, :]
            once = once + h
            twice = twice + once
            thrice = thrice + twice
        h0 = once
        h1 = 8.5 * once - twice
        h2 = 2.0 * thrice - 18.0 * twice + 72.25 * once
        u = iota((16, 1), 0).astype(F32) - 7.5

        def over(x):
            return jnp.sum(x, axis=0, keepdims=True)

        s["n"] = [over(h0), over(u * h0), over(h1), over(u * u * h0), over(u * h1), over(h2)]

    def scatter(s):
        cx, cy, a, b, c, _, _, _, opacity = s["fields"]
        rw = s["rw"]
        n00, n10, n01, n20, n11, n02 = s["n"]
        cu = cx - (s["ax"] + 8.0)
        cv = cy - (s["ay"] + 8.0)
        m10 = n10 - cu * n00
        m01 = n01 - cv * n00
        m20 = n20 - cu * (n10 + m10)
        m11 = n11 - cu * n01 - cv * m10
        m02 = n02 - cv * (n01 + m01)
        grads = [
            a * m10 + b * m01,
            b * m10 + c * m01,
            -0.5 * m20,
            -m11,
            -0.5 * m02,
            rw[0:1],
            rw[1:2],
            rw[2:3],
            n00 / opacity,
        ]
        mask = s["mask"].astype(BF16).reshape(2, 16, 256)
        for f in range(9):
            for piece, val in enumerate(split2(jnp.broadcast_to(grads[f], (16, 256)))):
                col = (2 * s["k"] + piece) * 256
                spread[s["g"], 32 * f : 32 * f + 32, col : col + 256] = (
                    mask * val[None]
                ).reshape(32, 256)

    def front(i):
        states = [
            {"b": TOGETHER * (i % 2) + k, "k": k, "g": i % 2, "t": i * TOGETHER + k}
            for k in range(TOGETHER)
        ]
        for s in states:
            gather(s)
        for s in states:
            pick(s)
            alphas(s)
        return states

    def back(states):
        slot = states[0]["g"]
        cum = dot(logs[slot], tri_le[...])
        for s in states:
            weights(s, cum)
        behind = dot(gw[slot], tri_gt[...])
        for s in states:
            slopes(s, behind)
            scatter(s)
        ones = []
        for s in states:
            ones += [s["one"], s["one"]]
        acc[...] += lax.dot_general(
            spread[slot],
            jnp.concatenate(ones, axis=1),
            (((1,), (1,)), ((), ())),
            preferred_element_type=F32,
        )

    steps = tiles // TOGETHER
    ready = front(0)
    for i in range(steps):
        following = front(i + 1) if i + 1 < steps else None
        back(ready)
        ready = following
    for f in range(9):
        for half in range(2):
            at = 64 * f + 32 * half
            turned[at : at + 32, :] = acc[32 * f : 32 * f + 32, 128 * half : 128 * half + 128]
    for q in range(5):
        out_ref[pl.ds(q, 128, stride=5), :] = turned[128 * q : 128 * q + 128, :].T


VMEM = pl.BlockSpec(memory_space=pltpu.VMEM)
SMEM = pl.BlockSpec(memory_space=pltpu.SMEM)
ON_CHIP = True


def held(x, interpret):
    if interpret or not ON_CHIP:
        return x
    return pltpu.with_memory_space_constraint(x, pltpu.VMEM)


def on_chip(shape, dtype, interpret):
    if interpret or not ON_CHIP:
        return jax.ShapeDtypeStruct(shape, dtype)
    return pltpu.VMEM(shape, dtype)


def block_shape(interpret):
    return on_chip((640, 128), F32, interpret)


def pack(device, tile_count, fields, rows, tile_list, light, interpret=False):
    return pl.pallas_call(
        pack_kernel,
        out_shape=[
            block_shape(interpret),
            on_chip((128, 128), jnp.int32, interpret),
            on_chip(tile_list.shape, jnp.int32, interpret),
            on_chip(light.shape, F32, interpret),
            on_chip((24, 256), F32, interpret),
        ],
        in_specs=[SMEM, SMEM, VMEM, VMEM, VMEM, VMEM],
        out_specs=[VMEM] * 5,
        scratch_shapes=[pltpu.VMEM((640, 128), F32)],
        name="pack",
        interpret=interpret,
    )(device, tile_count, fields, rows, tile_list, light)


def unpack(blocks, slots, interpret=False):
    return pl.pallas_call(
        unpack_kernel,
        out_shape=jax.ShapeDtypeStruct((9, 8192), F32),
        in_specs=[VMEM, VMEM],
        out_specs=VMEM,
        scratch_shapes=[pltpu.VMEM((640, 128), F32)],
        name="unpack",
        interpret=interpret,
    )(held(blocks, interpret), held(slots, interpret))


def tile_work(received, tile_list, light, tile_rows, interpret=False):
    both = 2 * TOGETHER
    return pl.pallas_call(
        tile_kernel,
        out_shape=block_shape(interpret),
        in_specs=[VMEM] * 4,
        out_specs=VMEM,
        scratch_shapes=[
            pltpu.VMEM((640, 128), F32),
            pltpu.VMEM((288, 512), BF16),
            pltpu.VMEM((64, 256), BF16),
            pltpu.VMEM((512, 256), BF16),
            pltpu.VMEM((512, 256), BF16),
            pltpu.VMEM((both, 352, 256), F32),
            pltpu.VMEM((2, 256 * TOGETHER, 512), BF16),
            pltpu.VMEM((both, 256, 256), F32),
            pltpu.VMEM((both, 256, 256), F32),
            pltpu.VMEM((2, 256 * TOGETHER, 512), BF16),
            pltpu.VMEM((both, 512, 256), BF16),
            pltpu.VMEM((2, 288, 512 * TOGETHER), BF16),
            pltpu.VMEM((288, 256), F32),
            pltpu.VMEM((256, 256), BF16),
        ],
        name="splat_tiles",
        interpret=interpret,
    )(*[held(x, interpret) for x in (received, tile_list, light, tile_rows)])


def exchange(blocks):
    moved = lax.all_to_all(
        blocks.reshape(128, 1, 640), AXES, split_axis=0, concat_axis=0, tiled=True
    )
    return moved.reshape(640, 128)


def on_device(gauss_fields, send_rows, tile_list, tile_count, pixel_grad):
    device = lax.axis_index(AXES).reshape(1).astype(jnp.int32)
    light = jnp.swapaxes(pixel_grad, 0, 1)
    blocks, slots, entries, light, tile_rows = pack(
        device, tile_count, gauss_fields, send_rows[0].T, tile_list, light
    )
    grads = tile_work(exchange(blocks), entries, light, tile_rows)
    return unpack(exchange(grads), slots)


def solution(mesh):
    placed = (
        P(None, AXES),
        P(AXES, None, None),
        P(AXES, None),
        P(AXES),
        P(AXES, None, None),
    )
    return jax.shard_map(
        on_device, mesh=mesh, in_specs=placed, out_specs=P(None, AXES), check_vma=False
    )
```

```python
import jax
import jax.numpy as jnp
from jax import lax
from jax.experimental import pallas as pl
from jax.experimental.pallas import tpu as pltpu
from jax.sharding import PartitionSpec as P

AXES = ("gauss", "pix")
TILES_X = 32
TILES_Y = 8
LOG2E = 1.4426950408889634
F32 = jnp.float32
BF16 = jnp.bfloat16
TOGETHER = 4
PITCH = 72


def split2(x):
    hi = x.astype(BF16)
    return hi, (x - hi.astype(F32)).astype(BF16)


def split3(x):
    hi = x.astype(BF16)
    rest = x - hi.astype(F32)
    mid = rest.astype(BF16)
    return hi, mid, (rest - mid.astype(F32)).astype(BF16)


def dot(a, b):
    return jnp.dot(a, b, preferred_element_type=F32)


def iota(shape, dim):
    return lax.broadcasted_iota(jnp.int32, shape, dim)


def pack_kernel(
    dev_ref, count_ref, fields_ref, rows_ref, list_ref, pg_ref,
    out_ref, slot_ref, list_out, pg_out, tile_out, grid_ref,
):
    list_out[...] = list_ref[...]
    pg_out[...] = pg_ref[...]
    tiles = list_ref.shape[0]
    for t in range(tiles):
        tile = dev_ref[0] * tiles + t
        live = iota((1, 256), 1) < count_ref[t]
        tile_out[t : t + 1, :] = jnp.where(live, 0.0, -100000.0)
        anchor_x = (tile % TILES_X * 16).astype(F32)
        anchor_y = (tile // TILES_X % TILES_Y * 16).astype(F32)
        tile_out[tiles + t : tiles + t + 1, :] = jnp.full((1, 256), anchor_x, F32)
        tile_out[2 * tiles + t : 2 * tiles + t + 1, :] = jnp.full((1, 256), anchor_y, F32)
    for p in range(64):
        lanes = slice(128 * p, 128 * p + 128)
        grid_ref[pl.ds(p, 8, stride=PITCH), :] = fields_ref[0:8, lanes]
        grid_ref[8 * PITCH + p : 8 * PITCH + p + 1, :] = fields_ref[8:9, lanes]
    grid_ref[9 * PITCH : 9 * PITCH + 64, :] = jnp.zeros((64, 128), F32)
    row = rows_ref[...] // 128
    order = jnp.concatenate([row, row + 64], axis=0).T
    for q in range(5):
        low, high = 2 * q * PITCH, (2 * q + 1) * PITCH
        block = jnp.concatenate(
            [grid_ref[low : low + 64, :], grid_ref[high : high + 64, :]], axis=0
        ).T
        out_ref[pl.ds(q, 128, stride=5), :] = jnp.take_along_axis(block, order, axis=1)
    place = iota((64, 128), 0)
    slot = jnp.zeros((64, 128), jnp.int32)
    for j in range(64):
        slot = jnp.where(row[j : j + 1, :] == place, j, slot)
    slot_ref[...] = jnp.concatenate([slot, slot + 64], axis=0).T


def unpack_kernel(in_ref, slot_ref, out_ref, grid_ref):
    order = slot_ref[...]
    for q in range(5):
        block = jnp.take_along_axis(in_ref[pl.ds(q, 128, stride=5), :], order, axis=1)
        turned = block.T
        low, high = 2 * q * PITCH, (2 * q + 1) * PITCH
        grid_ref[low : low + 64, :] = turned[0:64]
        grid_ref[high : high + 64, :] = turned[64:128]
    for p in range(64):
        lanes = slice(128 * p, 128 * p + 128)
        out_ref[0:8, lanes] = grid_ref[pl.ds(p, 8, stride=PITCH), :]
        out_ref[8:9, lanes] = grid_ref[8 * PITCH + p : 8 * PITCH + p + 1, :]


def tile_kernel(
    recv_ref, list_ref, pg_ref, tile_ref, out_ref,
    turned, rows, rows_lo, tri_le, tri_gt, found, logs, odds, part, gw, wts, spread, acc, place,
):
    tiles = list_ref.shape[0]
    for q in range(5):
        turned[128 * q : 128 * q + 128, :] = recv_ref[pl.ds(q, 128, stride=5), :].T
    for f in range(9):
        for half in range(2):
            at = slice(32 * f, 32 * f + 32)
            lane = 128 * half
            pieces = split3(turned[64 * f + 32 * half : 64 * f + 32 * half + 32, :])
            rows[at, lane : lane + 128] = pieces[0]
            rows[at, 256 + lane : 384 + lane] = pieces[1]
            if f < 2:
                rows_lo[at, lane : lane + 128] = pieces[2]
    before = (iota((256, 256), 0) <= iota((256, 256), 1)).astype(F32).astype(BF16)
    after = (iota((256, 256), 0) > iota((256, 256), 1)).astype(F32).astype(BF16)
    tri_le[0:256] = before
    tri_le[256:512] = before
    tri_gt[0:256] = after
    tri_gt[256:512] = after
    acc[...] = jnp.zeros_like(acc)
    place[...] = iota((256, 256), 0).astype(F32).astype(BF16)

    def gather(s):
        t = s["t"]
        s["ax"] = tile_ref[tiles + t : tiles + t + 1, :]
        s["ay"] = tile_ref[2 * tiles + t : 2 * tiles + t + 1, :]
        entry = list_ref[t : t + 1, :]
        key = (entry // 32) % 2 * 128 + entry // 64
        keys = jnp.broadcast_to(key.astype(F32), (16, 256)).astype(BF16)
        hit = place[...].reshape(16, 16, 256) == keys[None]
        s["one"] = jnp.where(hit, jnp.ones((), BF16), jnp.zeros((), BF16)).reshape(256, 256)
        s["mask"] = (iota((32, 256), 0) == entry % 32).astype(F32)
        found[s["b"], 0:288] = dot(rows[...], jnp.concatenate([s["one"], s["one"]], axis=0))
        found[s["b"], 288:352] = dot(rows_lo[...], s["one"])

    def pick(s):
        def field(f):
            block = s["mask"] * found[s["b"], 32 * f : 32 * f + 32, :]
            return jnp.sum(block, axis=0, keepdims=True)

        s["fields"] = [field(f) for f in range(9)]
        s["fields"][0] += field(9)
        s["fields"][1] += field(10)

    def alphas(s):
        b, k = s["b"], s["k"]
        cx, cy, a, b_, c, _, _, _, opacity = s["fields"]
        side = iota((16, 256), 0).astype(F32) + 0.5
        dx = (s["ax"] + side) - cx
        dy = (s["ay"] + side) - cy
        lead = jnp.log2(opacity) + tile_ref[s["t"] : s["t"] + 1, :]
        qa = (-0.5 * LOG2E) * a * dx * dx
        qb = -LOG2E * b_ * dx
        qc = (-0.5 * LOG2E) * c * dy * dy + lead
        for r in range(16):
            at = slice(16 * r, 16 * r + 16)
            e = qa + (qb * dy[r : r + 1, :] + qc[r : r + 1, :])
            alpha = jnp.exp2(e)
            kept = jnp.log2(1.0 - alpha)
            odds[b, at, :] = jnp.exp2(e - kept)
            lhi, llo = split2(kept)
            row = 256 * k + 16 * r
            logs[s["g"], row : row + 16, 0:256] = lhi
            logs[s["g"], row : row + 16, 256:512] = llo

    def weights(s, cum):
        b, k = s["b"], s["k"]
        chi, cmid = split2(jnp.concatenate(s["fields"][5:8], axis=0))
        light = jnp.concatenate([pg_ref[ch, s["t"] : s["t"] + 1, :] for ch in range(3)], axis=0)
        phi, pmid, plo = split3(light)
        zero = jnp.zeros((1, 256), BF16)
        colors = jnp.concatenate([chi, cmid, chi, cmid, chi, zero], axis=0)
        lights = jnp.concatenate([phi, phi, pmid, pmid, plo, zero], axis=0)
        g = lax.dot_general(lights, colors, (((0,), (0,)), ((), ())), preferred_element_type=F32)
        s["lit"] = jnp.concatenate([phi, pmid, plo, jnp.zeros((7, 256), BF16)], axis=0)
        for r in range(16):
            at = slice(16 * r, 16 * r + 16)
            w = jnp.exp2(cum[256 * k + 16 * r : 256 * k + 16 * r + 16]) * odds[b, at, :]
            whi, wlo = split2(w)
            wts[b, at, :] = whi
            wts[b, 256 + 16 * r : 272 + 16 * r, :] = wlo
            gpart = g[at] * w
            part[b, at, :] = gpart
            ghi, glo = split2(gpart)
            row = 256 * k + 16 * r
            gw[s["g"], row : row + 16, 0:256] = ghi
            gw[s["g"], row : row + 16, 256:512] = glo

    def slopes(s, behind):
        b, k = s["b"], s["k"]
        rw = dot(jnp.concatenate([s["lit"], s["lit"]], axis=1), wts[b])
        s["rw"] = rw[0:3] + rw[3:6] + rw[6:9]
        once = jnp.zeros((16, 256), F32)
        twice = jnp.zeros((16, 256), F32)
        thrice = jnp.zeros((16, 256), F32)
        for r in range(16):
            at = slice(16 * r, 16 * r + 16)
            row = 256 * k + 16 * r
            h = part[b, at, :] - behind[row : row + 16] * odds[b, at, :]
            once = once + h
            twice = twice + once
            thrice = thrice + twice
        h0 = once
        h1 = 8.5 * once - twice
        h2 = 2.0 * thrice - 18.0 * twice + 72.25 * once
        u = iota((16, 1), 0).astype(F32) - 7.5

        def over(x):
            return jnp.sum(x, axis=0, keepdims=True)

        s["n"] = [over(h0), over(u * h0), over(h1), over(u * u * h0), over(u * h1), over(h2)]

    def scatter(s):
        cx, cy, a, b, c, _, _, _, opacity = s["fields"]
        rw = s["rw"]
        n00, n10, n01, n20, n11, n02 = s["n"]
        cu = cx - (s["ax"] + 8.0)
        cv = cy - (s["ay"] + 8.0)
        m10 = n10 - cu * n00
        m01 = n01 - cv * n00
        m20 = n20 - cu * (n10 + m10)
        m11 = n11 - cu * n01 - cv * m10
        m02 = n02 - cv * (n01 + m01)
        grads = [
            a * m10 + b * m01,
            b * m10 + c * m01,
            -0.5 * m20,
            -m11,
            -0.5 * m02,
            rw[0:1],
            rw[1:2],
            rw[2:3],
            n00 / opacity,
        ]
        mask = s["mask"].astype(BF16).reshape(2, 16, 256)
        for f in range(9):
            for piece, val in enumerate(split2(jnp.broadcast_to(grads[f], (16, 256)))):
                col = (2 * s["k"] + piece) * 256
                spread[s["g"], 32 * f : 32 * f + 32, col : col + 256] = (
                    mask * val[None]
                ).reshape(32, 256)

    def begin(i):
        return [
            {"b": TOGETHER * (i % 2) + k, "k": k, "g": i % 2, "t": i * TOGETHER + k}
            for k in range(TOGETHER)
        ]

    def collect(states):
        ones = []
        for s in states:
            ones += [s["one"], s["one"]]
        acc[...] += lax.dot_general(
            spread[states[0]["g"]],
            jnp.concatenate(ones, axis=1),
            (((1,), (1,)), ((), ())),
            preferred_element_type=F32,
        )

    def each(phase, states, *more):
        for s in states:
            phase(s, *more)

    def prepare(s):
        pick(s)
        alphas(s)

    steps = tiles // TOGETHER
    now = begin(0)
    each(gather, now)
    each(prepare, now)
    for i in range(steps):
        slot = i % 2
        later = begin(i + 1) if i + 1 < steps else []
        cum = dot(logs[slot], tri_le[...])
        each(gather, later)
        each(weights, now, cum)
        behind = dot(gw[slot], tri_gt[...])
        each(prepare, later)
        each(slopes, now, behind)
        each(scatter, now)
        collect(now)
        now = later
    for f in range(9):
        for half in range(2):
            at = 64 * f + 32 * half
            turned[at : at + 32, :] = acc[32 * f : 32 * f + 32, 128 * half : 128 * half + 128]
    for q in range(5):
        out_ref[pl.ds(q, 128, stride=5), :] = turned[128 * q : 128 * q + 128, :].T


VMEM = pl.BlockSpec(memory_space=pltpu.VMEM)
SMEM = pl.BlockSpec(memory_space=pltpu.SMEM)
ON_CHIP = True


def held(x, interpret):
    if interpret or not ON_CHIP:
        return x
    return pltpu.with_memory_space_constraint(x, pltpu.VMEM)


def on_chip(shape, dtype, interpret):
    if interpret or not ON_CHIP:
        return jax.ShapeDtypeStruct(shape, dtype)
    return pltpu.VMEM(shape, dtype)


def block_shape(interpret):
    return on_chip((640, 128), F32, interpret)


def pack(device, tile_count, fields, rows, tile_list, light, interpret=False):
    return pl.pallas_call(
        pack_kernel,
        out_shape=[
            block_shape(interpret),
            on_chip((128, 128), jnp.int32, interpret),
            on_chip(tile_list.shape, jnp.int32, interpret),
            on_chip(light.shape, F32, interpret),
            on_chip((24, 256), F32, interpret),
        ],
        in_specs=[SMEM, SMEM, VMEM, VMEM, VMEM, VMEM],
        out_specs=[VMEM] * 5,
        scratch_shapes=[pltpu.VMEM((10 * PITCH, 128), F32)],
        name="pack",
        interpret=interpret,
    )(device, tile_count, fields, rows, tile_list, light)


def unpack(blocks, slots, interpret=False):
    return pl.pallas_call(
        unpack_kernel,
        out_shape=jax.ShapeDtypeStruct((9, 8192), F32),
        in_specs=[VMEM, VMEM],
        out_specs=VMEM,
        scratch_shapes=[pltpu.VMEM((10 * PITCH, 128), F32)],
        name="unpack",
        interpret=interpret,
    )(held(blocks, interpret), held(slots, interpret))


def tile_work(received, tile_list, light, tile_rows, interpret=False):
    both = 2 * TOGETHER
    return pl.pallas_call(
        tile_kernel,
        out_shape=block_shape(interpret),
        in_specs=[VMEM] * 4,
        out_specs=VMEM,
        scratch_shapes=[
            pltpu.VMEM((640, 128), F32),
            pltpu.VMEM((288, 512), BF16),
            pltpu.VMEM((64, 256), BF16),
            pltpu.VMEM((512, 256), BF16),
            pltpu.VMEM((512, 256), BF16),
            pltpu.VMEM((both, 352, 256), F32),
            pltpu.VMEM((2, 256 * TOGETHER, 512), BF16),
            pltpu.VMEM((both, 256, 256), F32),
            pltpu.VMEM((both, 256, 256), F32),
            pltpu.VMEM((2, 256 * TOGETHER, 512), BF16),
            pltpu.VMEM((both, 512, 256), BF16),
            pltpu.VMEM((2, 288, 512 * TOGETHER), BF16),
            pltpu.VMEM((288, 256), F32),
            pltpu.VMEM((256, 256), BF16),
        ],
        name="splat_tiles",
        interpret=interpret,
    )(*[held(x, interpret) for x in (received, tile_list, light, tile_rows)])


def exchange(blocks):
    moved = lax.all_to_all(
        blocks.reshape(128, 1, 640), AXES, split_axis=0, concat_axis=0, tiled=True
    )
    return moved.reshape(640, 128)


def on_device(gauss_fields, send_rows, tile_list, tile_count, pixel_grad):
    device = lax.axis_index(AXES).reshape(1).astype(jnp.int32)
    light = jnp.swapaxes(pixel_grad, 0, 1)
    blocks, slots, entries, light, tile_rows = pack(
        device, tile_count, gauss_fields, send_rows[0].T, tile_list, light
    )
    grads = tile_work(exchange(blocks), entries, light, tile_rows)
    return unpack(exchange(grads), slots)


def solution(mesh):
    placed = (
        P(None, AXES),
        P(AXES, None, None),
        P(AXES, None),
        P(AXES),
        P(AXES, None, None),
    )
    return jax.shard_map(
        on_device, mesh=mesh, in_specs=placed, out_specs=P(None, AXES), check_vma=False
    )
```

```python
import jax
import jax.numpy as jnp
from jax import lax
from jax.experimental import pallas as pl
from jax.experimental.pallas import tpu as pltpu
from jax.sharding import PartitionSpec as P

AXES = ("gauss", "pix")
TILES_X = 32
TILES_Y = 8
LOG2E = 1.4426950408889634
F32 = jnp.float32
BF16 = jnp.bfloat16
TOGETHER = 4
PITCH = 72


def split2(x):
    hi = x.astype(BF16)
    return hi, (x - hi.astype(F32)).astype(BF16)


def split3(x):
    hi = x.astype(BF16)
    rest = x - hi.astype(F32)
    mid = rest.astype(BF16)
    return hi, mid, (rest - mid.astype(F32)).astype(BF16)


def dot(a, b):
    return jnp.dot(a, b, preferred_element_type=F32)


def iota(shape, dim):
    return lax.broadcasted_iota(jnp.int32, shape, dim)


def pack_kernel(
    dev_ref, count_ref, fields_ref, rows_ref, list_ref, pg_ref,
    out_ref, slot_ref, list_out, pg_out, tile_out, grid_ref,
):
    list_out[...] = list_ref[...]
    pg_out[...] = pg_ref[...]
    tiles = list_ref.shape[0]
    for t in range(tiles):
        tile = dev_ref[0] * tiles + t
        live = iota((1, 256), 1) < count_ref[t]
        tile_out[t : t + 1, :] = jnp.where(live, 0.0, -100000.0)
        anchor_x = (tile % TILES_X * 16).astype(F32)
        anchor_y = (tile // TILES_X % TILES_Y * 16).astype(F32)
        tile_out[tiles + t : tiles + t + 1, :] = jnp.full((1, 256), anchor_x, F32)
        tile_out[2 * tiles + t : 2 * tiles + t + 1, :] = jnp.full((1, 256), anchor_y, F32)
    for p in range(64):
        lanes = slice(128 * p, 128 * p + 128)
        grid_ref[pl.ds(p, 8, stride=PITCH), :] = fields_ref[0:8, lanes]
        grid_ref[8 * PITCH + p : 8 * PITCH + p + 1, :] = fields_ref[8:9, lanes]
    grid_ref[9 * PITCH : 9 * PITCH + 64, :] = jnp.zeros((64, 128), F32)
    row = rows_ref[...] // 128
    order = jnp.concatenate([row, row + 64], axis=0).T
    for q in range(5):
        low, high = 2 * q * PITCH, (2 * q + 1) * PITCH
        block = jnp.concatenate(
            [grid_ref[low : low + 64, :], grid_ref[high : high + 64, :]], axis=0
        ).T
        out_ref[pl.ds(q, 128, stride=5), :] = jnp.take_along_axis(block, order, axis=1)
    place = iota((64, 128), 0).astype(F32).astype(BF16).reshape(4, 16, 128)
    wanted = row.astype(F32)
    slot = jnp.zeros((4, 16, 128), BF16)
    for j in range(64):
        here = jnp.broadcast_to(wanted[j : j + 1, :], (16, 128)).astype(BF16)
        slot = jnp.where(place == here[None], jnp.full((), j, BF16), slot)
    slot = slot.reshape(64, 128).astype(F32).astype(jnp.int32)
    slot_ref[...] = jnp.concatenate([slot, slot + 64], axis=0).T


def unpack_kernel(in_ref, slot_ref, out_ref, grid_ref):
    order = slot_ref[...]
    for q in range(5):
        block = jnp.take_along_axis(in_ref[pl.ds(q, 128, stride=5), :], order, axis=1)
        turned = block.T
        low, high = 2 * q * PITCH, (2 * q + 1) * PITCH
        grid_ref[low : low + 64, :] = turned[0:64]
        grid_ref[high : high + 64, :] = turned[64:128]
    for p in range(64):
        lanes = slice(128 * p, 128 * p + 128)
        out_ref[0:8, lanes] = grid_ref[pl.ds(p, 8, stride=PITCH), :]
        out_ref[8:9, lanes] = grid_ref[8 * PITCH + p : 8 * PITCH + p + 1, :]


def tile_kernel(
    recv_ref, list_ref, pg_ref, tile_ref, out_ref,
    turned, rows, rows_lo, tri_le, tri_gt, found, logs, odds, part, gw, wts, spread, acc, place,
):
    tiles = list_ref.shape[0]
    for q in range(5):
        turned[128 * q : 128 * q + 128, :] = recv_ref[pl.ds(q, 128, stride=5), :].T
    for f in range(9):
        for half in range(2):
            at = slice(32 * f, 32 * f + 32)
            lane = 128 * half
            pieces = split3(turned[64 * f + 32 * half : 64 * f + 32 * half + 32, :])
            rows[at, lane : lane + 128] = pieces[0]
            rows[at, 256 + lane : 384 + lane] = pieces[1]
            if f < 2:
                rows_lo[at, lane : lane + 128] = pieces[2]
    before = (iota((256, 256), 0) <= iota((256, 256), 1)).astype(F32).astype(BF16)
    after = (iota((256, 256), 0) > iota((256, 256), 1)).astype(F32).astype(BF16)
    tri_le[0:256] = before
    tri_le[256:512] = before
    tri_gt[0:256] = after
    tri_gt[256:512] = after
    acc[...] = jnp.zeros_like(acc)
    place[...] = iota((256, 256), 0).astype(F32).astype(BF16)

    def gather(s):
        t = s["t"]
        s["ax"] = tile_ref[tiles + t : tiles + t + 1, :]
        s["ay"] = tile_ref[2 * tiles + t : 2 * tiles + t + 1, :]
        entry = list_ref[t : t + 1, :]
        key = (entry // 32) % 2 * 128 + entry // 64
        keys = jnp.broadcast_to(key.astype(F32), (16, 256)).astype(BF16)
        hit = place[...].reshape(16, 16, 256) == keys[None]
        s["one"] = jnp.where(hit, jnp.ones((), BF16), jnp.zeros((), BF16)).reshape(256, 256)
        s["mask"] = (iota((32, 256), 0) == entry % 32).astype(F32)
        found[s["b"], 0:288] = dot(rows[...], jnp.concatenate([s["one"], s["one"]], axis=0))
        found[s["b"], 288:352] = dot(rows_lo[...], s["one"])

    def pick(s):
        def field(f):
            block = s["mask"] * found[s["b"], 32 * f : 32 * f + 32, :]
            return jnp.sum(block, axis=0, keepdims=True)

        s["fields"] = [field(f) for f in range(9)]
        s["fields"][0] += field(9)
        s["fields"][1] += field(10)

    def alphas(s):
        b, k = s["b"], s["k"]
        cx, cy, a, b_, c, _, _, _, opacity = s["fields"]
        side = iota((16, 256), 0).astype(F32) + 0.5
        dx = (s["ax"] + side) - cx
        dy = (s["ay"] + side) - cy
        lead = jnp.log2(opacity) + tile_ref[s["t"] : s["t"] + 1, :]
        qa = (-0.5 * LOG2E) * a * dx * dx
        qb = -LOG2E * b_ * dx
        qc = (-0.5 * LOG2E) * c * dy * dy + lead
        for r in range(16):
            at = slice(16 * r, 16 * r + 16)
            e = qa + (qb * dy[r : r + 1, :] + qc[r : r + 1, :])
            alpha = jnp.exp2(e)
            kept = jnp.log2(1.0 - alpha)
            odds[b, at, :] = jnp.exp2(e - kept)
            lhi, llo = split2(kept)
            row = 256 * k + 16 * r
            logs[s["g"], row : row + 16, 0:256] = lhi
            logs[s["g"], row : row + 16, 256:512] = llo

    def weights(s, cum):
        b, k = s["b"], s["k"]
        chi, cmid = split2(jnp.concatenate(s["fields"][5:8], axis=0))
        light = jnp.concatenate([pg_ref[ch, s["t"] : s["t"] + 1, :] for ch in range(3)], axis=0)
        phi, pmid, plo = split3(light)
        zero = jnp.zeros((1, 256), BF16)
        colors = jnp.concatenate([chi, cmid, chi, cmid, chi, zero], axis=0)
        lights = jnp.concatenate([phi, phi, pmid, pmid, plo, zero], axis=0)
        g = lax.dot_general(lights, colors, (((0,), (0,)), ((), ())), preferred_element_type=F32)
        s["lit"] = jnp.concatenate([phi, pmid, plo, jnp.zeros((7, 256), BF16)], axis=0)
        for r in range(16):
            at = slice(16 * r, 16 * r + 16)
            w = jnp.exp2(cum[256 * k + 16 * r : 256 * k + 16 * r + 16]) * odds[b, at, :]
            whi, wlo = split2(w)
            wts[b, at, :] = whi
            wts[b, 256 + 16 * r : 272 + 16 * r, :] = wlo
            gpart = g[at] * w
            part[b, at, :] = gpart
            ghi, glo = split2(gpart)
            row = 256 * k + 16 * r
            gw[s["g"], row : row + 16, 0:256] = ghi
            gw[s["g"], row : row + 16, 256:512] = glo

    def slopes(s, behind):
        b, k = s["b"], s["k"]
        rw = dot(jnp.concatenate([s["lit"], s["lit"]], axis=1), wts[b])
        s["rw"] = rw[0:3] + rw[3:6] + rw[6:9]
        once = jnp.zeros((16, 256), F32)
        twice = jnp.zeros((16, 256), F32)
        thrice = jnp.zeros((16, 256), F32)
        for r in range(16):
            at = slice(16 * r, 16 * r + 16)
            row = 256 * k + 16 * r
            h = part[b, at, :] - behind[row : row + 16] * odds[b, at, :]
            once = once + h
            twice = twice + once
            thrice = thrice + twice
        h0 = once
        h1 = 8.5 * once - twice
        h2 = 2.0 * thrice - 18.0 * twice + 72.25 * once
        u = iota((16, 1), 0).astype(F32) - 7.5

        def over(x):
            return jnp.sum(x, axis=0, keepdims=True)

        s["n"] = [over(h0), over(u * h0), over(h1), over(u * u * h0), over(u * h1), over(h2)]

    def scatter(s):
        cx, cy, a, b, c, _, _, _, opacity = s["fields"]
        rw = s["rw"]
        n00, n10, n01, n20, n11, n02 = s["n"]
        cu = cx - (s["ax"] + 8.0)
        cv = cy - (s["ay"] + 8.0)
        m10 = n10 - cu * n00
        m01 = n01 - cv * n00
        m20 = n20 - cu * (n10 + m10)
        m11 = n11 - cu * n01 - cv * m10
        m02 = n02 - cv * (n01 + m01)
        grads = [
            a * m10 + b * m01,
            b * m10 + c * m01,
            -0.5 * m20,
            -m11,
            -0.5 * m02,
            rw[0:1],
            rw[1:2],
            rw[2:3],
            n00 / opacity,
        ]
        mask = s["mask"].astype(BF16).reshape(2, 16, 256)
        for f in range(9):
            for piece, val in enumerate(split2(jnp.broadcast_to(grads[f], (16, 256)))):
                col = (2 * s["k"] + piece) * 256
                spread[s["g"], 32 * f : 32 * f + 32, col : col + 256] = (
                    mask * val[None]
                ).reshape(32, 256)

    def begin(i):
        return [
            {"b": TOGETHER * (i % 2) + k, "k": k, "g": i % 2, "t": i * TOGETHER + k}
            for k in range(TOGETHER)
        ]

    def collect(states):
        ones = []
        for s in states:
            ones += [s["one"], s["one"]]
        acc[...] += lax.dot_general(
            spread[states[0]["g"]],
            jnp.concatenate(ones, axis=1),
            (((1,), (1,)), ((), ())),
            preferred_element_type=F32,
        )

    def each(phase, states, *more):
        for s in states:
            phase(s, *more)

    def prepare(s):
        pick(s)
        alphas(s)

    steps = tiles // TOGETHER
    now = begin(0)
    each(gather, now)
    each(prepare, now)
    for i in range(steps):
        slot = i % 2
        later = begin(i + 1) if i + 1 < steps else []
        cum = dot(logs[slot], tri_le[...])
        each(gather, later)
        each(weights, now, cum)
        behind = dot(gw[slot], tri_gt[...])
        each(prepare, later)
        each(slopes, now, behind)
        each(scatter, now)
        collect(now)
        now = later
    for f in range(9):
        for half in range(2):
            at = 64 * f + 32 * half
            turned[at : at + 32, :] = acc[32 * f : 32 * f + 32, 128 * half : 128 * half + 128]
    for q in range(5):
        out_ref[pl.ds(q, 128, stride=5), :] = turned[128 * q : 128 * q + 128, :].T


VMEM = pl.BlockSpec(memory_space=pltpu.VMEM)
SMEM = pl.BlockSpec(memory_space=pltpu.SMEM)
ON_CHIP = True


def held(x, interpret):
    if interpret or not ON_CHIP:
        return x
    return pltpu.with_memory_space_constraint(x, pltpu.VMEM)


def on_chip(shape, dtype, interpret):
    if interpret or not ON_CHIP:
        return jax.ShapeDtypeStruct(shape, dtype)
    return pltpu.VMEM(shape, dtype)


def block_shape(interpret):
    return on_chip((640, 128), F32, interpret)


def pack(device, tile_count, fields, rows, tile_list, light, interpret=False):
    return pl.pallas_call(
        pack_kernel,
        out_shape=[
            block_shape(interpret),
            on_chip((128, 128), jnp.int32, interpret),
            on_chip(tile_list.shape, jnp.int32, interpret),
            on_chip(light.shape, F32, interpret),
            on_chip((24, 256), F32, interpret),
        ],
        in_specs=[SMEM, SMEM, VMEM, VMEM, VMEM, VMEM],
        out_specs=[VMEM] * 5,
        scratch_shapes=[pltpu.VMEM((10 * PITCH, 128), F32)],
        name="pack",
        interpret=interpret,
    )(device, tile_count, fields, rows, tile_list, light)


def unpack(blocks, slots, interpret=False):
    return pl.pallas_call(
        unpack_kernel,
        out_shape=jax.ShapeDtypeStruct((9, 8192), F32),
        in_specs=[VMEM, VMEM],
        out_specs=VMEM,
        scratch_shapes=[pltpu.VMEM((10 * PITCH, 128), F32)],
        name="unpack",
        interpret=interpret,
    )(held(blocks, interpret), held(slots, interpret))


def tile_work(received, tile_list, light, tile_rows, interpret=False):
    both = 2 * TOGETHER
    return pl.pallas_call(
        tile_kernel,
        out_shape=block_shape(interpret),
        in_specs=[VMEM] * 4,
        out_specs=VMEM,
        scratch_shapes=[
            pltpu.VMEM((640, 128), F32),
            pltpu.VMEM((288, 512), BF16),
            pltpu.VMEM((64, 256), BF16),
            pltpu.VMEM((512, 256), BF16),
            pltpu.VMEM((512, 256), BF16),
            pltpu.VMEM((both, 352, 256), F32),
            pltpu.VMEM((2, 256 * TOGETHER, 512), BF16),
            pltpu.VMEM((both, 256, 256), F32),
            pltpu.VMEM((both, 256, 256), F32),
            pltpu.VMEM((2, 256 * TOGETHER, 512), BF16),
            pltpu.VMEM((both, 512, 256), BF16),
            pltpu.VMEM((2, 288, 512 * TOGETHER), BF16),
            pltpu.VMEM((288, 256), F32),
            pltpu.VMEM((256, 256), BF16),
        ],
        name="splat_tiles",
        interpret=interpret,
    )(*[held(x, interpret) for x in (received, tile_list, light, tile_rows)])


def exchange(blocks):
    moved = lax.all_to_all(
        blocks.reshape(128, 1, 640), AXES, split_axis=0, concat_axis=0, tiled=True
    )
    return moved.reshape(640, 128)


def on_device(gauss_fields, send_rows, tile_list, tile_count, pixel_grad):
    device = lax.axis_index(AXES).reshape(1).astype(jnp.int32)
    light = jnp.swapaxes(pixel_grad, 0, 1)
    blocks, slots, entries, light, tile_rows = pack(
        device, tile_count, gauss_fields, send_rows[0].T, tile_list, light
    )
    grads = tile_work(exchange(blocks), entries, light, tile_rows)
    return unpack(exchange(grads), slots)


def solution(mesh):
    placed = (
        P(None, AXES),
        P(AXES, None, None),
        P(AXES, None),
        P(AXES),
        P(AXES, None, None),
    )
    return jax.shard_map(
        on_device, mesh=mesh, in_specs=placed, out_specs=P(None, AXES), check_vma=False
    )
```
